32 devices in a mesh: dp: 16 (over z, y, x), tensor: 2 (over core).
Axes of the slice: x: 2, y: 2, z: 4, core: 2. Of those that a mesh axis runs over, the one named last changes fastest.
Arguments:
- tokens: bfloat16 [16384, 768], P('dp'), may hold values from -6 to 6
- cotangent: bfloat16 [16384, 768], P('dp'), may hold values from -6 to 6
- w_query: bfloat16 [768, 768], P(None, 'tensor'), may hold values from -0.3125 to 0.3125
- b_query: float32 [768], P('tensor'), may hold values from -3 to 3
- w_key: bfloat16 [768, 768], P(None, 'tensor'), may hold values from -0.3125 to 0.3125
- w_value: bfloat16 [768, 768], P(None, 'tensor'), may hold values from -0.21875 to 0.21875
- b_value: float32 [768], P('tensor'), may hold values from -3 to 3
- w_out: bfloat16 [768, 768], P('tensor'), may hold values from -0.875 to 0.875
- b_out: float32 [768], replicated, may hold values from -3 to 3
- w_in: bfloat16 [768, 3072], P(None, 'tensor'), may hold values from -0.21875 to 0.21875
- b_in: float32 [3072], P('tensor'), may hold values from -3 to 3
- w_back: bfloat16 [3072, 768], P('tensor'), may hold values from -0.21875 to 0.21875
- b_back: float32 [768], replicated, may hold values from -3 to 3
- gain_attn: float32 [768], replicated, may hold values from 0.5 to 1.5
- shift_attn: float32 [768], replicated, may hold values from -2 to 2
- gain_ffn: float32 [768], replicated, may hold values from 0.5 to 1.5
- shift_ffn: float32 [768], replicated, may hold values from -2 to 2
Outputs:
- block_out: bfloat16 [16384, 768], P('dp')
- grad_tokens: float32 [16384, 768], P('dp')
- grad_w_query: float32 [768, 768], P(None, 'tensor')
- grad_b_query: float32 [768], P('tensor')
- grad_w_key: float32 [768, 768], P(None, 'tensor')
- grad_w_value: float32 [768, 768], P(None, 'tensor')
- grad_b_value: float32 [768], P('tensor')
- grad_w_out: float32 [768, 768], P('tensor')
- grad_b_out: float32 [768], replicated
- grad_w_in: float32 [768, 3072], P(None, 'tensor')
- grad_b_in: float32 [3072], P('tensor')
- grad_w_back: float32 [3072, 768], P('tensor')
- grad_b_back: float32 [768], replicated
- grad_gain_attn: float32 [768], replicated
- grad_shift_attn: float32 [768], replicated
- grad_gain_ffn: float32 [768], replicated
- grad_shift_ffn: float32 [768], replicated
The draws below stay inside these ranges and needn't reach their ends.
All inputs are finite; a program needn't handle non-finite values.
Results may differ from the reference program's by a relative error of at most 0.015.
The reference program's roundings to bfloat16 on the way count: a program that leaves them out, or rounds other values in their place, can miss the bound.
Values may be sent and summed in bfloat16 or wider, within the bound.
A program may use at most 192 MiB of HBM per device.

```python
import jax
import jax.numpy as jnp
from jax import lax

D = 768
FF = 3072
HEADS = 12
HEAD = 64
SEQ = 512
TOKENS = 16384


def block_scale(key, extent, cuts, low, top_value):
    level = 1.0
    for position, parts in cuts:
        steps = jax.random.uniform(jax.random.fold_in(jax.random.fold_in(key, 6), position), (parts,), jnp.float32, low / len(cuts), top_value / len(cuts))
        level = level * jnp.repeat(jnp.exp(steps), extent[position] // parts).reshape((-1,) + (1,) * (len(extent) - 1 - position))
    return level


def noise(own_key, shape, width, bound, pieces=(), held_as=jnp.bfloat16):
    entries = width * jax.random.normal(own_key, shape, jnp.float32)
    if pieces:
        entries = entries * block_scale(own_key, shape, pieces, -0.22, 0.18)
    return jnp.clip(entries, -bound, bound).astype(held_as)


def setup_inputs(seed: int = 0) -> dict:
    arg_keys = jax.random.split(jax.random.key(seed), 18)
    return {
        "tokens": noise(arg_keys[0], (TOKENS, D), 1.0, 6.0, ((0, 16),)),
        "cotangent": noise(arg_keys[1], (TOKENS, D), 1.0, 6.0, ((0, 16),)),
        "w_query": noise(arg_keys[2], (D, D), (D // 2) ** -0.5, 0.3125, ((1, 2),)),
        "b_query": noise(arg_keys[3], (D,), 0.5, 3.0, ((0, 2),), jnp.float32),
        "w_key": noise(arg_keys[4], (D, D), (D // 2) ** -0.5, 0.3125, ((1, 2),)),
        "w_value": noise(arg_keys[5], (D, D), D ** -0.5, 0.21875, ((1, 2),)),
        "b_value": noise(arg_keys[6], (D,), 0.5, 3.0, ((0, 2),), jnp.float32),
        "w_out": noise(arg_keys[7], (D, D), (D // 16) ** -0.5, 0.875, ((0, 2),)),
        "b_out": noise(arg_keys[8], (D,), 0.5, 3.0, (), jnp.float32),
        "w_in": noise(arg_keys[9], (D, FF), D ** -0.5, 0.21875, ((1, 2),)),
        "b_in": noise(arg_keys[10], (FF,), 0.5, 3.0, ((0, 2),), jnp.float32),
        "w_back": noise(arg_keys[11], (FF, D), (FF // 4) ** -0.5, 0.21875, ((0, 2),)),
        "b_back": noise(arg_keys[12], (D,), 0.5, 3.0, (), jnp.float32),
        "gain_attn": jnp.clip(1.0 + 0.1 * jax.random.normal(arg_keys[13], (D,), jnp.float32), 0.5, 1.5),
        "shift_attn": noise(arg_keys[14], (D,), 0.3, 2.0, (), jnp.float32),
        "gain_ffn": jnp.clip(1.0 + 0.1 * jax.random.normal(arg_keys[15], (D,), jnp.float32), 0.5, 1.5),
        "shift_ffn": noise(arg_keys[16], (D,), 0.3, 2.0, (), jnp.float32),
    }


EPS = 1e-12
HIGH = lax.Precision.HIGHEST

@jax.custom_vjp
def low(v):
    return lax.optimization_barrier(v.astype(jnp.bfloat16)).astype(jnp.float32)

@jax.custom_vjp
def low_back(v):
    return v

def low_keep(v):
    return (low(v), None)

def low_pass(kept, grad):
    return (grad,)

def back_keep(v):
    return (v, None)

def back_low(kept, grad):
    return (low(grad),)
low.defvjp(low_keep, low_pass)
low_back.defvjp(back_keep, back_low)

def layer_norm(v, gain, shift):
    mean = lax.optimization_barrier(jnp.mean(v, axis=-1, keepdims=True))
    centred = v - mean
    var = lax.optimization_barrier(jnp.mean(centred * centred, axis=-1, keepdims=True))
    return centred * lax.rsqrt(var + EPS) * gain + shift

def block(xg, params):
    w_query, b_query, w_key, w_value, b_value, w_out, b_out, w_in, b_in, w_back, b_back, gain_attn, shift_attn, gain_ffn, shift_ffn = params
    group, length = (xg.shape[0], xg.shape[1])
    normed = low(layer_norm(xg, gain_attn, shift_attn))
    query = low(low_back(jnp.matmul(normed, w_query, precision=HIGH) + b_query))
    key = low(low_back(jnp.matmul(normed, w_key, precision=HIGH)))
    value = low(low_back(jnp.matmul(normed, w_value, precision=HIGH) + b_value))
    query = query.reshape(group, length, HEADS, HEAD)
    key = key.reshape(group, length, HEADS, HEAD)
    value = value.reshape(group, length, HEADS, HEAD)
    scores = low_back(jnp.einsum('gqhd,gkhd->ghqk', query, key, precision=HIGH) * HEAD ** (-0.5))
    top = lax.optimization_barrier(jnp.max(scores, axis=-1, keepdims=True))
    expo = jnp.exp(scores - top)
    probs = low(expo / lax.optimization_barrier(jnp.sum(expo, axis=-1, keepdims=True)))
    mixed = jnp.einsum('ghqk,gkhd->gqhd', probs, value, precision=HIGH).reshape(group, length, D)
    mixed = low(low_back(mixed))
    attn = low_back(jnp.matmul(mixed, w_out, precision=HIGH) + b_out)
    hidden = xg + attn
    normed2 = low(layer_norm(hidden, gain_ffn, shift_ffn))
    pre = low_back(jnp.matmul(normed2, w_in, precision=HIGH) + b_in)
    act = low(jax.nn.gelu(pre, approximate=False))
    ffn = low_back(jnp.matmul(act, w_back, precision=HIGH) + b_back)
    return hidden + ffn

def forward(xf, params):
    bundle = 8
    groups = xf.reshape(-1, bundle, SEQ, D)

    def stepper(carry, xg):
        return (carry, jax.checkpoint(block)(xg, params))
    unused, outs = lax.scan(stepper, jnp.float32(0.0), groups)
    return outs.reshape(-1, D)

def reference(tokens, cotangent, w_query, b_query, w_key, w_value, b_value, w_out, b_out, w_in, b_in, w_back, b_back, gain_attn, shift_attn, gain_ffn, shift_ffn):
    params = tuple((item.astype(jnp.float32) for item in (w_query, b_query, w_key, w_value, b_value, w_out, b_out, w_in, b_in, w_back, b_back, gain_attn, shift_attn, gain_ffn, shift_ffn)))
    xf = tokens.astype(jnp.float32)
    result, pullback = jax.vjp(forward, xf, params)
    grad_x, grads = pullback(cotangent.astype(jnp.float32))
    return (result.astype(jnp.bfloat16), grad_x, grads[0], grads[1], grads[2], grads[3], grads[4], grads[5], grads[6], grads[7], grads[8], grads[9], grads[10], grads[11], grads[12], grads[13], grads[14])
```

```python
import functools

import jax
import jax.numpy as jnp
from jax import lax
from jax.experimental import pallas as pl
from jax.experimental.pallas import tpu as pltpu
from jax.sharding import PartitionSpec as P

HEAD = 64
SEQ = 512


EPS = 1e-12


def matmul(left, right):
    return jnp.dot(left, right, preferred_element_type=jnp.float32)


def matmul_left(left, right):
    return lax.dot_general(
        left, right, (((0,), (0,)), ((), ())), preferred_element_type=jnp.float32
    )


def matmul_right(left, right):
    return lax.dot_general(
        left, right, (((1,), (1,)), ((), ())), preferred_element_type=jnp.float32
    )


def norm_parts(value, gain, shift):
    mean = jnp.mean(value, axis=-1, keepdims=True)
    centred = value - mean
    rstd = lax.rsqrt(jnp.mean(centred * centred, axis=-1, keepdims=True) + EPS)
    unit = centred * rstd
    return (unit * gain + shift, unit, rstd)


def norm_back(grad_out, unit, rstd, gain):
    scaled = grad_out * gain
    return rstd * (
        scaled
        - jnp.mean(scaled, axis=-1, keepdims=True)
        - unit * jnp.mean(scaled * unit, axis=-1, keepdims=True)
    )


def gelu_slope(pre):
    return (
        0.5 * (1.0 + lax.erf(pre * 0.7071067811865476))
        + pre * jnp.exp(-0.5 * pre * pre) * 0.3989422804014327
    )


WIDE = 256


def strides_of(bits, colour, step):
    low = [1 << bit for bit in range(bits)]
    if bits < 3:
        orders = [low, low, low]
    else:
        orders = [low, [low[1], low[0]] + low[2:], low[2:] + low[:2]]
    first, second, third = orders[0][step], orders[1][step], orders[2][step]
    return jnp.where(colour == 0, first, jnp.where(colour == 1, second, third))


def colour_of(piece):
    return lax.rem(piece, 3)


def reduce_kernel(bits, pieces, lag, grads, out, held, landed, load_sem, send_sem, recv_sem, free_sem, out_sem):
    me = lax.axis_index("dp")
    rows = held.shape[1]

    def bit_at(colour, step):
        stride = strides_of(bits, colour, step)
        return stride, lax.rem(lax.div(me, stride), 2)

    def partner_of(piece, step):
        stride, bit = bit_at(colour_of(piece), step)
        return me + (1 - 2 * bit) * stride

    def region(colour, step):
        base = 0
        for earlier in range(step):
            base = base + bit_at(colour, earlier)[1] * (rows >> (earlier + 1))
        return base

    def load(piece):
        return pltpu.make_async_copy(grads.at[piece], held.at[piece], load_sem.at[piece])

    def store(piece):
        return pltpu.make_async_copy(held.at[piece], out.at[piece], out_sem.at[piece])

    def copy(piece, step):
        colour = colour_of(piece)
        level = step if step < bits else 2 * bits - 1 - step
        stride, bit = bit_at(colour, level)
        partner = me + (1 - 2 * bit) * stride
        half = rows >> (level + 1)
        base = region(colour, level)
        if step < bits:
            start = pl.multiple_of(base + (1 - bit) * half, 16)
            source = held.at[piece, pl.ds(start, half)]
            target = landed.at[piece, pl.ds(rows - (rows >> level), half)]
        else:
            start = pl.multiple_of(base + bit * half, 16)
            source = held.at[piece, pl.ds(start, half)]
            target = held.at[piece, pl.ds(start, half)]
        return pltpu.make_async_remote_copy(
            src_ref=source,
            dst_ref=target,
            send_sem=send_sem.at[piece, step],
            recv_sem=recv_sem.at[piece, step],
            device_id={"dp": partner},
            device_id_type=pl.DeviceIdType.MESH,
        )

    def add(piece, step):
        colour = colour_of(piece)
        bit = bit_at(colour, step)[1]
        half = rows >> (step + 1)
        start = pl.multiple_of(region(colour, step) + bit * half, 16)
        mine = held[piece, pl.ds(start, half)].astype(jnp.float32)
        other = landed[piece, pl.ds(rows - (rows >> step), half)].astype(jnp.float32)
        held[piece, pl.ds(start, half)] = (mine + other).astype(held.dtype)

    def advance(piece, step):
        if step == 0:
            load(piece).wait()
        else:
            copy(piece, step - 1).wait_recv()
            if step <= bits:
                copy(piece, step - 1).wait_send()
                pl.semaphore_signal(
                    free_sem.at[piece, step - 1],
                    inc=1,
                    device_id={"dp": partner_of(piece, step - 1)},
                    device_id_type=pl.DeviceIdType.MESH,
                )
                add(piece, step - 1)
        if step < 2 * bits:
            if step >= bits:
                pl.semaphore_wait(free_sem.at[piece, 2 * bits - 1 - step], 1)
            copy(piece, step).start()
        else:
            store(piece).start()

    barrier = pltpu.get_barrier_semaphore()
    for bit in range(bits):
        mine = lax.rem(lax.div(me, 1 << bit), 2)
        pl.semaphore_signal(
            barrier,
            inc=1,
            device_id={"dp": me + (1 - 2 * mine) * (1 << bit)},
            device_id_type=pl.DeviceIdType.MESH,
        )

    def begin(piece, carry):
        load(piece).start()
        return carry

    lax.fori_loop(0, pieces, begin, 0)
    pl.semaphore_wait(barrier, bits)

    def tick(time, carry):
        for step in range(2 * bits + 1):
            piece = time - lag * step

            @pl.when((piece >= 0) & (piece < pieces))
            def _():
                advance(piece, step)

        return carry

    lax.fori_loop(0, pieces + lag * 2 * bits, tick, 0)

    def finish(piece, carry):
        for step in range(bits, 2 * bits):
            copy(piece, step).wait_send()
        store(piece).wait()
        return carry

    lax.fori_loop(0, pieces, finish, 0)


def reduce_pieces(grads, count):
    pieces, rows, wide = grads.shape
    bits = count.bit_length() - 1
    return pl.pallas_call(
        functools.partial(reduce_kernel, bits, pieces, LAG),
        out_shape=jax.ShapeDtypeStruct(grads.shape, grads.dtype),
        in_specs=[pl.BlockSpec(memory_space=pl.ANY)],
        out_specs=pl.BlockSpec(memory_space=pl.ANY),
        scratch_shapes=[
            pltpu.VMEM((pieces, rows, wide), grads.dtype),
            pltpu.VMEM((pieces, rows - (rows >> bits), wide), grads.dtype),
            pltpu.SemaphoreType.DMA((pieces,)),
            pltpu.SemaphoreType.DMA((pieces, 2 * bits)),
            pltpu.SemaphoreType.DMA((pieces, 2 * bits)),
            pltpu.SemaphoreType.REGULAR((pieces, bits)),
            pltpu.SemaphoreType.DMA((pieces,)),
        ],
        compiler_params=pltpu.CompilerParams(
            collective_id=0, has_side_effects=True, vmem_limit_bytes=48 << 20
        ),
        name="reduce_pieces",
    )(grads)


LAG = 2


def to_pieces(matrix):
    rows, columns = matrix.shape
    return matrix.reshape(rows, columns // WIDE, WIDE).transpose(1, 0, 2)


def from_pieces(pieces):
    count, rows, wide = pieces.shape
    return pieces.transpose(1, 0, 2).reshape(rows, count * wide)


def one_batch(x_rows, cot_rows, params):
    (
        w_query,
        b_query,
        w_key,
        w_value,
        b_value,
        w_out,
        b_out,
        w_in,
        b_in,
        w_back,
        b_back,
        gain_attn,
        shift_attn,
        gain_ffn,
        shift_ffn,
    ) = params
    local = w_query.shape[1]
    heads_here = local // HEAD
    scale = HEAD ** (-0.5)
    length = x_rows.shape[0]
    seqs = length // SEQ
    share = length // lax.axis_size("tensor")
    offset = lax.axis_index("tensor") * share
    xf = x_rows.astype(jnp.float32)
    x_share = lax.dynamic_slice_in_dim(xf, offset, share, 0)
    normed_f, unit_one, rstd_one = norm_parts(xf, gain_attn, shift_attn)
    normed = normed_f.astype(jnp.bfloat16)
    query = (
        (matmul(normed, w_query) + b_query).astype(jnp.bfloat16).reshape(seqs, SEQ, heads_here, HEAD)
    )
    key = matmul(normed, w_key).astype(jnp.bfloat16).reshape(seqs, SEQ, heads_here, HEAD)
    value = (
        (matmul(normed, w_value) + b_value).astype(jnp.bfloat16).reshape(seqs, SEQ, heads_here, HEAD)
    )
    scores = jnp.einsum("bqhd,bkhd->bhqk", query, key, preferred_element_type=jnp.float32) * scale
    top = jnp.max(scores, axis=-1, keepdims=True)
    expo = jnp.exp(scores - top)
    total = jnp.sum(expo, axis=-1, keepdims=True)
    log_total = top + jnp.log(total)
    probs = expo / total
    mixed = (
        jnp.einsum(
            "bhqk,bkhd->bqhd", probs.astype(jnp.bfloat16), value, preferred_element_type=jnp.float32
        )
        .reshape(length, local)
        .astype(jnp.bfloat16)
    )
    attn_share = (
        lax.psum_scatter(matmul(mixed, w_out), "tensor", scatter_dimension=0, tiled=True) + b_out
    )
    hidden_share = x_share + attn_share
    normed2_f, unit_two, rstd_two = norm_parts(hidden_share, gain_ffn, shift_ffn)
    normed2 = lax.all_gather(normed2_f.astype(jnp.bfloat16), "tensor", axis=0, tiled=True)
    pre = matmul(normed2, w_in) + b_in
    act = jax.nn.gelu(pre, approximate=False).astype(jnp.bfloat16)
    ffn_share = (
        lax.psum_scatter(
            matmul(act, w_back).astype(jnp.bfloat16), "tensor", scatter_dimension=0, tiled=True
        ).astype(jnp.float32)
        + b_back
    )
    result = lax.all_gather(
        (hidden_share + ffn_share).astype(jnp.bfloat16), "tensor", axis=0, tiled=True
    )
    grad_y = cot_rows.astype(jnp.float32)
    dy_share = lax.dynamic_slice_in_dim(grad_y, offset, share, 0)
    g_b_back = jnp.sum(grad_y, axis=0)
    g_w_back = matmul_left(cot_rows, act)
    dpre = (matmul_right(cot_rows, w_back) * gelu_slope(pre)).astype(jnp.bfloat16)
    g_b_in = jnp.sum(dpre.astype(jnp.float32), axis=0)
    g_w_in = matmul_left(normed2, dpre)
    dnormed2 = lax.psum_scatter(matmul_right(dpre, w_in), "tensor", scatter_dimension=0, tiled=True)
    part_gain_ffn = jnp.sum(dnormed2 * unit_two, axis=0)
    part_shift_ffn = jnp.sum(dnormed2, axis=0)
    dhidden_share = dy_share + norm_back(dnormed2, unit_two, rstd_two, gain_ffn)
    dattn = lax.all_gather(dhidden_share.astype(jnp.bfloat16), "tensor", axis=0, tiled=True)
    g_b_out = jnp.sum(dattn.astype(jnp.float32), axis=0)
    g_w_out = matmul_left(dattn, mixed)
    dmixed = matmul_right(dattn, w_out).astype(jnp.bfloat16).reshape(seqs, SEQ, heads_here, HEAD)
    again = jnp.einsum("bqhd,bkhd->bhqk", query, key, preferred_element_type=jnp.float32) * scale
    probs_again = jnp.exp(again - log_total)
    dprobs = jnp.einsum("bqhd,bkhd->bhqk", dmixed, value, preferred_element_type=jnp.float32)
    dscores = (
        probs_again * (dprobs - jnp.sum(dprobs * probs_again, axis=-1, keepdims=True))
    ).astype(jnp.bfloat16)
    dquery = (
        (jnp.einsum("bhqk,bkhd->bqhd", dscores, key, preferred_element_type=jnp.float32) * scale)
        .reshape(length, local)
        .astype(jnp.bfloat16)
    )
    dkey = (
        (jnp.einsum("bhqk,bqhd->bkhd", dscores, query, preferred_element_type=jnp.float32) * scale)
        .reshape(length, local)
        .astype(jnp.bfloat16)
    )
    dvalue = (
        jnp.einsum(
            "bhqk,bqhd->bkhd",
            probs_again.astype(jnp.bfloat16),
            dmixed,
            preferred_element_type=jnp.float32,
        )
        .reshape(length, local)
        .astype(jnp.bfloat16)
    )
    g_b_query = jnp.sum(dquery.astype(jnp.float32), axis=0)
    g_b_value = jnp.sum(dvalue.astype(jnp.float32), axis=0)
    g_w_query = matmul_left(normed, dquery)
    g_w_key = matmul_left(normed, dkey)
    g_w_value = matmul_left(normed, dvalue)
    dnormed = lax.psum_scatter(
        (
            matmul_right(dquery, w_query)
            + matmul_right(dkey, w_key)
            + matmul_right(dvalue, w_value)
        ).astype(jnp.bfloat16),
        "tensor",
        scatter_dimension=0,
        tiled=True,
    ).astype(jnp.float32)
    unit_one_share = lax.dynamic_slice_in_dim(unit_one, offset, share, 0)
    rstd_one_share = lax.dynamic_slice_in_dim(rstd_one, offset, share, 0)
    part_gain_attn = jnp.sum(dnormed * unit_one_share, axis=0)
    part_shift_attn = jnp.sum(dnormed, axis=0)
    grad_share = dhidden_share + norm_back(dnormed, unit_one_share, rstd_one_share, gain_attn)
    grad_x = lax.all_gather(grad_share.astype(jnp.bfloat16), "tensor", axis=0, tiled=True).astype(
        grad_share.dtype
    )
    g_gain_ffn, g_shift_ffn, g_gain_attn, g_shift_attn = lax.psum(
        (part_gain_ffn, part_shift_ffn, part_gain_attn, part_shift_attn), "tensor"
    )
    grads = (
        g_w_query,
        g_b_query,
        g_w_key,
        g_w_value,
        g_b_value,
        g_w_out,
        g_b_out,
        g_w_in,
        g_b_in,
        g_w_back,
        g_b_back,
        g_gain_attn,
        g_shift_attn,
        g_gain_ffn,
        g_shift_ffn,
    )
    return (result, grad_x, grads)


def on_device(
    tokens,
    cotangent,
    w_query,
    b_query,
    w_key,
    w_value,
    b_value,
    w_out,
    b_out,
    w_in,
    b_in,
    w_back,
    b_back,
    gain_attn,
    shift_attn,
    gain_ffn,
    shift_ffn,
):
    width = tokens.shape[1]
    params = (
        w_query,
        b_query,
        w_key,
        w_value,
        b_value,
        w_out,
        b_out,
        w_in,
        b_in,
        w_back,
        b_back,
        gain_attn,
        shift_attn,
        gain_ffn,
        shift_ffn,
    )
    count = lax.axis_size("dp")
    results, grad_rows, grads = one_batch(tokens, cotangent, params)
    (g_wq, g_bq, g_wk, g_wv, g_bv, g_wo, g_bo, g_wi, g_bi, g_wb, g_bb, g_ga, g_sa, g_gf, g_sf) = grads
    vectors = (g_bq, g_bv, g_bo, g_bi, g_bb, g_ga, g_sa, g_gf, g_sf)
    sizes = [item.shape[0] for item in vectors]
    summed = lax.psum(jnp.concatenate(vectors), "dp")
    bounds = [sum(sizes[:i]) for i in range(len(sizes) + 1)]
    r_bq, r_bv, r_bo, r_bi, r_bb, r_ga, r_sa, r_gf, r_sf = (
        summed[bounds[i] : bounds[i + 1]] for i in range(len(sizes))
    )
    whole = jnp.concatenate([g_wi, g_wb, g_wq, g_wk, g_wv, g_wo], axis=1).astype(jnp.bfloat16)
    if width % (16 * count) == 0 and count & (count - 1) == 0:
        whole = from_pieces(reduce_pieces(to_pieces(whole), count))
    else:
        whole = lax.psum(whole, "dp")
    whole = whole.astype(jnp.float32)
    cuts = [0]
    for item in (g_wi, g_wb, g_wq, g_wk, g_wv, g_wo):
        cuts.append(cuts[-1] + item.shape[1])
    r_wi, r_wb, r_wq, r_wk, r_wv, r_wo = (whole[:, cuts[i] : cuts[i + 1]] for i in range(6))
    return (
        results,
        grad_rows,
        r_wq,
        r_bq,
        r_wk,
        r_wv,
        r_bv,
        r_wo.T,
        r_bo,
        r_wi,
        r_bi,
        r_wb.T,
        r_bb,
        r_ga,
        r_sa,
        r_gf,
        r_sf,
    )


def solution(mesh):
    return jax.shard_map(
        on_device,
        mesh=mesh,
        in_specs=(
            P("dp", None),
            P("dp", None),
            P(None, "tensor"),
            P("tensor"),
            P(None, "tensor"),
            P(None, "tensor"),
            P("tensor"),
            P("tensor", None),
            P(),
            P(None, "tensor"),
            P("tensor"),
            P("tensor", None),
            P(),
            P(),
            P(),
            P(),
            P(),
        ),
        out_specs=(
            P("dp", None),
            P("dp", None),
            P(None, "tensor"),
            P("tensor"),
            P(None, "tensor"),
            P(None, "tensor"),
            P("tensor"),
            P("tensor", None),
            P(),
            P(None, "tensor"),
            P("tensor"),
            P("tensor", None),
            P(),
            P(),
            P(),
            P(),
            P(),
        ),
        check_vma=False,
    )
```

```python
import functools

import jax
import jax.numpy as jnp
from jax import lax
from jax.experimental import pallas as pl
from jax.experimental.pallas import tpu as pltpu
from jax.sharding import PartitionSpec as P

HEAD = 64
SEQ = 512
EPS = 1e-12
SHARDS = 16
ROWS = 48
LANES = 128
LAG = 2
MESH = pl.DeviceIdType.MESH
F32 = jnp.float32
BF16 = jnp.bfloat16


def matmul(left, right):
    return jnp.dot(left, right, preferred_element_type=F32)


def matmul_left(left, right):
    return lax.dot_general(left, right, (((0,), (0,)), ((), ())), preferred_element_type=F32)


def matmul_right(left, right):
    return lax.dot_general(left, right, (((1,), (1,)), ((), ())), preferred_element_type=F32)


def norm_parts(value):
    mean = jnp.mean(value, axis=-1, keepdims=True)
    centred = value - mean
    rstd = lax.rsqrt(jnp.mean(centred * centred, axis=-1, keepdims=True) + EPS)
    return centred * rstd, rstd


def norm_back(scaled, unit, rstd):
    return rstd * (
        scaled
        - jnp.mean(scaled, axis=-1, keepdims=True)
        - unit * jnp.mean(scaled * unit, axis=-1, keepdims=True)
    )


def fold(value):
    return jnp.sum(value.reshape(value.shape[0] // 8, 8, value.shape[1]), axis=0)


class Sizes:
    def __init__(self, count, tokens, w_query, w_in):
        self.count = count
        self.bits = count.bit_length() - 1
        self.halving = min(self.bits, SHARDS.bit_length() - 1)
        self.sends = self.bits + self.halving
        self.width = tokens.shape[1]
        self.local = w_query.shape[1]
        self.hidden = w_in.shape[1]
        self.chunks = self.hidden // self.width
        self.block = self.width // LANES
        self.per_chunk = 2 * self.block
        self.first_out = self.chunks * self.per_chunk
        self.first_qkv = self.first_out + self.local // LANES
        self.pieces = self.first_qkv + 3 * self.local // LANES
        self.landing = SHARDS - (SHARDS >> self.halving) + self.bits - self.halving


def bit_orders(bits, halving):
    low = list(range(halving))
    high = list(range(halving, bits))
    if halving < 3:
        return [low + high] * 3
    return [low + high, [1, 0] + low[2:] + high, low[2:] + low[:2] + high]


def layer_kernel(
    size,
    tokens,
    cotangent,
    w_query,
    w_key,
    w_value,
    w_out,
    w_in,
    w_back,
    b_query,
    b_value,
    b_out,
    b_in,
    b_back,
    gain_attn,
    shift_attn,
    gain_ffn,
    shift_ffn,
    out_rows,
    out_grad,
    out_pieces,
    out_vectors,
    wqkv,
    wo,
    wi,
    wb,
    bias_q,
    bias_v,
    bias_i,
    x_s,
    dy_s,
    normed,
    qkv,
    mixed,
    lse,
    hidden,
    normed2,
    flip2,
    ffn,
    dn2,
    act,
    dpre,
    flip,
    wide_a,
    wide_b,
    dattn,
    dmixed,
    result,
    probs_t,
    dscores_t,
    held,
    other,
    pair,
    landed,
    vec,
    vec_other,
    vec_landed,
    load_sem,
    weight_send,
    weight_recv,
    pair_send,
    pair_recv,
    send_sem,
    recv_sem,
    free_sem,
    store_sem,
    vec_send,
    vec_recv,
    row_send,
    row_recv,
    row_sem,
):
    me = lax.axis_index("dp")
    core = lax.axis_index("tensor")
    width, local = size.width, size.local
    bits, halving, sends, pieces = size.bits, size.halving, size.sends, size.pieces
    orders = bit_orders(bits, halving)
    my_rows = pl.ds(pl.multiple_of(core * SEQ, SEQ), SEQ)

    def colour_of(piece):
        place = lax.rem(piece, 13)
        third = (place == 4) | (place == 8) | (place == 12)
        return jnp.where(third, 2, lax.rem(place, 2))

    def bit_at(colour, level):
        strides = [1 << order[level] for order in orders]
        stride = jnp.where(
            colour == 0, strides[0], jnp.where(colour == 1, strides[1], strides[2])
        )
        return stride, lax.rem(lax.div(me, stride), 2)

    def partner_of(colour, level):
        stride, bit = bit_at(colour, level)
        return me + (1 - 2 * bit) * stride

    def base_of(colour, level):
        base = 0
        for earlier in range(min(level, halving)):
            base = base + bit_at(colour, earlier)[1] * (SHARDS >> (earlier + 1))
        return base

    def landing_of(level):
        if level < halving:
            return SHARDS - (SHARDS >> level), SHARDS >> (level + 1)
        return SHARDS - (SHARDS >> halving) + level - halving, SHARDS >> halving

    def level_of(step):
        return step if step < bits else sends - 1 - step

    def copy(piece, step):
        colour = colour_of(piece)
        level = level_of(step)
        stride, bit = bit_at(colour, level)
        base = base_of(colour, level)
        if level < halving:
            half = SHARDS >> (level + 1)
            start = base + ((1 - bit) if step < bits else bit) * half
        else:
            half = SHARDS >> halving
            start = base
        source = held.at[piece, pl.ds(start, half)]
        target = source
        if step < bits:
            target = landed.at[piece, pl.ds(landing_of(level)[0], half)]
        return pltpu.make_async_remote_copy(
            src_ref=source,
            dst_ref=target,
            send_sem=send_sem.at[piece, step],
            recv_sem=recv_sem.at[piece, step],
            device_id={"dp": me + (1 - 2 * bit) * stride},
            device_id_type=MESH,
        )

    def add_level(piece, level):
        colour = colour_of(piece)
        base = base_of(colour, level + 1)
        place, half = landing_of(level)

        def one(shard, carry):
            mine = held[piece, base + shard].astype(F32)
            theirs = landed[piece, place + shard].astype(F32)
            held[piece, base + shard] = (mine + theirs).astype(BF16)
            return carry

        lax.fori_loop(0, half, one, 0)

    def pair_copy(piece):
        return pltpu.make_async_remote_copy(
            src_ref=other.at[piece],
            dst_ref=pair.at[piece],
            send_sem=pair_send.at[piece],
            recv_sem=pair_recv.at[piece],
            device_id={"tensor": 1 - core},
            device_id_type=MESH,
        )

    def store(piece):
        return pltpu.make_async_copy(held.at[piece], out_pieces.at[piece], store_sem.at[piece])

    def advance(piece, step):
        if step == 0:
            pair_copy(piece).wait_recv()

            def one(shard, carry):
                mine = held[piece, shard].astype(F32)
                held[piece, shard] = (mine + pair[piece, shard].astype(F32)).astype(BF16)
                return carry

            lax.fori_loop(0, SHARDS, one, 0)
        else:
            copy(piece, step - 1).wait_recv()
            if step <= bits:
                copy(piece, step - 1).wait_send()
                if step <= halving:
                    pl.semaphore_signal(
                        free_sem.at[piece, step - 1],
                        inc=1,
                        device_id={"dp": partner_of(colour_of(piece), step - 1)},
                        device_id_type=MESH,
                    )
                add_level(piece, step - 1)
        if step < sends:
            if step >= bits:
                pl.semaphore_wait(free_sem.at[piece, level_of(step)], 1)
            copy(piece, step).start()
        else:
            store(piece).start()

    def tick(time, carry):
        for step in range(sends + 1):
            piece = time - LAG * step

            @pl.when((piece >= 0) & (piece < pieces))
            def _():
                advance(piece, step)

        return carry

    def ticks(first, amount):
        lax.fori_loop(first, first + amount, tick, 0)

    def send_pairs(first, amount):
        def one(piece, carry):
            pair_copy(piece).start()
            return carry

        lax.fori_loop(first, first + amount, one, 0)

    def load(source, target, place):
        return pltpu.make_async_copy(source, target, load_sem.at[place])

    loads = [
        load(tokens.at[my_rows], x_s, 0),
        load(cotangent.at[my_rows], dy_s, 1),
        load(w_query, wqkv.at[0, :, pl.ds(0, local)], 2),
        load(w_key, wqkv.at[0, :, pl.ds(local, local)], 3),
        load(w_value, wqkv.at[0, :, pl.ds(2 * local, local)], 4),
        load(w_out, wo.at[pl.ds(0, local)], 5),
        load(w_in, wi.at[0], 6),
        load(w_back, wb.at[0], 7),
    ]
    for item in loads:
        item.start()

    barrier = pltpu.get_barrier_semaphore()
    pl.semaphore_signal(barrier, inc=1, device_id={"tensor": 1 - core}, device_id_type=MESH)
    for bit in range(bits):
        mine = lax.rem(lax.div(me, 1 << bit), 2)
        pl.semaphore_signal(
            barrier,
            inc=1,
            device_id={"dp": me + (1 - 2 * mine) * (1 << bit)},
            device_id_type=MESH,
        )
    pl.semaphore_wait(barrier, bits + 1)

    def to_partner(source, target, place):
        return pltpu.make_async_remote_copy(
            src_ref=source,
            dst_ref=target,
            send_sem=weight_send.at[place],
            recv_sem=weight_recv.at[place],
            device_id={"tensor": 1 - core},
            device_id_type=MESH,
        )

    gathers = [
        to_partner(b_query, bias_q, 0),
        to_partner(b_value, bias_v, 1),
        to_partner(b_in, bias_i, 2),
        to_partner(w_query, wqkv.at[1, :, pl.ds(0, local)], 3),
        to_partner(w_key, wqkv.at[1, :, pl.ds(local, local)], 4),
        to_partner(w_value, wqkv.at[1, :, pl.ds(2 * local, local)], 5),
        to_partner(w_out, wo.at[pl.ds(local, local)], 6),
        to_partner(w_in, wi.at[1], 7),
        to_partner(w_back, wb.at[1], 8),
    ]
    for item in gathers:
        item.start()

    vec[...] = jnp.zeros_like(vec)
    vec_other[...] = jnp.zeros_like(vec_other)
    ffn[...] = jnp.zeros_like(ffn)
    dn2[...] = jnp.zeros_like(dn2)

    small = 64
    loads[0].wait()

    def first_norm(tile, carry):
        rows = pl.ds(pl.multiple_of(tile * small, small), small)
        unit, rstd = norm_parts(x_s[rows].astype(F32))
        normed[rows] = (unit * gain_attn[...] + shift_attn[...]).astype(BF16)
        return carry

    lax.fori_loop(0, SEQ // small, first_norm, 0)

    for half in range(2):
        if half == 0:
            for item in loads[2:5]:
                item.wait()
            bias_query, bias_value = b_query, b_value
        else:
            for item in gathers[0:2] + gathers[3:6]:
                item.wait_recv()
            bias_query, bias_value = bias_q, bias_v
        qkv[half, :, 0:local] = (
            matmul(normed[...], wqkv[half, :, 0:local]) + bias_query[...]
        ).astype(BF16)
        qkv[half, :, local : 2 * local] = matmul(
            normed[...], wqkv[half, :, local : 2 * local]
        ).astype(BF16)
        qkv[half, :, 2 * local : 3 * local] = (
            matmul(normed[...], wqkv[half, :, 2 * local : 3 * local]) + bias_value[...]
        ).astype(BF16)

    pairs_half = local // LANES
    scale = HEAD ** (-0.5)
    lane = lax.broadcasted_iota(jnp.int32, (1, LANES), 1)
    masks = [
        jnp.where((lane >= part * HEAD) & (lane < (part + 1) * HEAD), 1.0, 0.0).astype(BF16)
        for part in range(LANES // HEAD)
    ]
    queries = 128

    def columns(index, group):
        return pl.ds(pl.multiple_of(group * local + index * LANES, LANES), LANES)

    def attend(index, carry):
        half, place = lax.div(index, pairs_half), lax.rem(index, pairs_half)
        key = qkv[half, :, columns(place, 1)]
        value = qkv[half, :, columns(place, 2)]
        total = None
        for part, mask in enumerate(masks):
            for tile in range(SEQ // queries):
                rows = slice(tile * queries, (tile + 1) * queries)
                query = qkv[half, rows, columns(place, 0)] * (mask * scale).astype(BF16)
                scores = matmul_right(key, query)
                top = jnp.max(scores, axis=0, keepdims=True)
                expo = jnp.exp(scores - top)
                amount = jnp.sum(expo, axis=0, keepdims=True)
                lse[index * 2 + part, :, rows] = top + jnp.log(amount)
                probs_t[part, :, rows] = (expo * (1.0 / amount)).astype(BF16)
            term = matmul_left(probs_t[part], value * mask)
            total = term if total is None else total + term
        mixed[:, pl.ds(pl.multiple_of(index * LANES, LANES), LANES)] = total.astype(BF16)
        return carry

    lax.fori_loop(0, 2 * pairs_half, attend, 0)

    loads[5].wait()
    gathers[6].wait_recv()
    hidden[...] = matmul(mixed[...], wo[...])

    def second_norm(tile, carry):
        rows = pl.ds(pl.multiple_of(tile * small, small), small)
        whole = x_s[rows].astype(F32) + (hidden[rows] + b_out[...])
        hidden[rows] = whole
        unit, rstd = norm_parts(whole)
        normed2[rows] = (unit * gain_ffn[...] + shift_ffn[...]).astype(BF16)
        return carry

    lax.fori_loop(0, SEQ // small, second_norm, 0)
    flip2[...] = normed2[...].T

    loads[1].wait()
    loads[6].wait()
    loads[7].wait()
    gathers[2].wait_recv()
    gathers[7].wait_recv()
    gathers[8].wait_recv()
    ones = jnp.ones((16, SEQ), BF16)
    fine = 32
    tall = 256

    def hand_in(target, first, grad, kind, part):
        wide = 2 * LANES
        if kind == "in":
            for side in range(2):
                target[first + 2 * part + side] = (
                    grad[:, side * LANES : (side + 1) * LANES]
                    .astype(BF16)
                    .reshape(SHARDS, ROWS, LANES)
                )
        else:
            blocks = grad.shape[0] // (ROWS * SHARDS // 2)
            for block in range(blocks):
                rows = slice(block * ROWS * SHARDS // 2, (block + 1) * ROWS * SHARDS // 2)
                for side in range(2):
                    target[
                        first + (width // wide) * block + part,
                        side * (SHARDS // 2) : (side + 1) * (SHARDS // 2),
                    ] = (
                        grad[rows, side * LANES : (side + 1) * LANES]
                        .astype(BF16)
                        .reshape(SHARDS // 2, ROWS, LANES)
                    )

    def feed(chunk, half, slots):
        begin = pl.multiple_of(chunk * width, width)
        units = pl.ds(begin, width)
        bias_row = b_in if half == 0 else bias_i
        target = held if half == 0 else other
        first = chunk * size.per_chunk

        def rows_tile(tile, carry):
            rows = pl.ds(pl.multiple_of(tile * tall, tall), tall)
            wide_a[...] = matmul(normed2[rows], wi[half, :, units])
            wide_b[...] = matmul_right(dy_s[rows], wb[half, units, :])

            def inner(step, carry):
                piece = pl.ds(pl.multiple_of(step * fine, fine), fine)
                there = pl.ds(pl.multiple_of(tile * tall + step * fine, fine), fine)
                pre = wide_a[piece] + bias_row[:, units]
                phi = 0.5 * (1.0 + lax.erf(pre * 0.7071067811865476))
                act[there] = (pre * phi).astype(BF16)
                slope = phi + pre * jnp.exp(-0.5 * pre * pre) * 0.3989422804014327
                dpre[there] = (wide_b[piece] * slope).astype(BF16)
                return carry

            lax.fori_loop(0, tall // fine, inner, 0)
            return carry

        lax.fori_loop(0, SEQ // tall, rows_tile, 0)
        slots(0)
        flip[...] = act[...].T
        ffn[...] += matmul(act[...], wb[half, units, :])
        slots(1)
        dn2[...] += matmul_right(dpre[...], wi[half, :, units])
        slots(2)
        for part in range(width // 256):
            cols = slice(part * 256, (part + 1) * 256)
            hand_in(target, first, matmul(flip2[...], dpre[:, cols]), "in", part)
        slots(3)
        for part in range(width // 256):
            cols = slice(part * 256, (part + 1) * 256)
            hand_in(target, first + size.block, matmul(flip[...], dy_s[:, cols]), "out", part)
        slots(4)
        sums = matmul(ones, dpre[...])[0:1]
        (vec if half == 0 else vec_other)[pl.ds(7 + chunk, 1)] = sums

    def feed_both(chunk, carry):
        def slots(offset):
            def place(index):
                first = (chunk - 1) * 10 + offset + index
                lax.fori_loop(first, jnp.where(chunk > 0, first + 1, first), tick, 0)

            return place

        feed(chunk, 1, slots(0))
        send_pairs(chunk * size.per_chunk, size.per_chunk)
        feed(chunk, 0, slots(5))
        return carry

    lax.fori_loop(0, size.chunks, feed_both, 0)
    time = 10 * (size.chunks - 1)

    tiny = 32

    def second_back(tile, carry):
        sum_gain, sum_shift, sum_out = carry
        rows = pl.ds(pl.multiple_of(tile * tiny, tiny), tiny)
        whole = hidden[rows]
        result[rows] = (whole + (ffn[rows] + b_back[...])).astype(BF16)
        unit, rstd = norm_parts(whole)
        grad = dn2[rows]
        dhidden = dy_s[rows].astype(F32) + norm_back(grad * gain_ffn[...], unit, rstd)
        dn2[rows] = dhidden
        rounded = dhidden.astype(BF16)
        dattn[rows] = rounded
        return (
            sum_gain + fold(grad * unit),
            sum_shift + fold(grad),
            sum_out + fold(rounded.astype(F32)),
        )

    zero = jnp.zeros((8, width), F32)
    sum_gain, sum_shift, sum_out = lax.fori_loop(
        0, SEQ // tiny, second_back, (zero, zero, zero)
    )

    def both(row, value):
        vec[row : row + 1] = value
        vec_other[row : row + 1] = value

    both(0, jnp.sum(sum_out, axis=0, keepdims=True))
    both(1, matmul(ones, dy_s[...])[0:1])
    both(4, jnp.sum(sum_gain, axis=0, keepdims=True))
    both(5, jnp.sum(sum_shift, axis=0, keepdims=True))

    def row_copies(source, target, place):
        return (
            pltpu.make_async_copy(source, target.at[my_rows], row_sem.at[place]),
            pltpu.make_async_remote_copy(
                src_ref=source,
                dst_ref=target.at[my_rows],
                send_sem=row_send.at[place],
                recv_sem=row_recv.at[place],
                device_id={"tensor": 1 - core},
                device_id_type=MESH,
            ),
        )

    result_copies = row_copies(result, out_rows, 0)
    for item in result_copies:
        item.start()
    ticks(time, 2)
    time += 2

    flip[...] = mixed[...].T
    for part in range(width // 256):
        cols = slice(part * 256, (part + 1) * 256)
        grad = matmul(flip[...], dattn[:, cols])
        hand_in(held, size.first_out, grad[0:local], "out", part)
        hand_in(other, size.first_out, grad[local:], "out", part)
    send_pairs(size.first_out, size.first_qkv - size.first_out)
    dmixed[...] = matmul_right(dattn[...], wo[...]).astype(BF16)
    ticks(time, 1)
    time += 1

    def attend_back(index, carry):
        half, place = lax.div(index, pairs_half), lax.rem(index, pairs_half)
        here = pl.ds(pl.multiple_of(index * LANES, LANES), LANES)
        key = qkv[half, :, columns(place, 1)]
        value = qkv[half, :, columns(place, 2)]
        dquery, dkey, dvalue = None, None, None
        for part, mask in enumerate(masks):
            for tile in range(SEQ // queries):
                rows = slice(tile * queries, (tile + 1) * queries)
                query = qkv[half, rows, columns(place, 0)] * (mask * scale).astype(BF16)
                scores = matmul_right(key, query)
                probs = jnp.exp(scores - lse[index * 2 + part, :, rows])
                dprobs = matmul_right(value, dmixed[rows, here] * mask)
                inner = jnp.sum(dprobs * probs, axis=0, keepdims=True)
                probs_t[part, :, rows] = probs.astype(BF16)
                dscores_t[part, :, rows] = (probs * (dprobs - inner)).astype(BF16)
            query = qkv[half, :, columns(place, 0)] * (mask * scale).astype(BF16)
            terms = (
                matmul_left(dscores_t[part], key * mask),
                matmul(dscores_t[part], query),
                matmul(probs_t[part], dmixed[:, here] * mask),
            )
            if dquery is None:
                dquery, dkey, dvalue = terms
            else:
                dquery, dkey, dvalue = dquery + terms[0], dkey + terms[1], dvalue + terms[2]
        qkv[half, :, columns(place, 0)] = (dquery * scale).astype(BF16)
        qkv[half, :, columns(place, 1)] = dkey.astype(BF16)
        qkv[half, :, columns(place, 2)] = dvalue.astype(BF16)
        ticks(time + 2 * index, 2)
        return carry

    lax.fori_loop(0, 2 * pairs_half, attend_back, 0)
    time += 4 * pairs_half

    flip[...] = normed[...].T
    for half in (1, 0):
        target = held if half == 0 else other
        for part in range(3 * local // LANES):
            cols = slice(part * LANES, (part + 1) * LANES)
            grad = matmul(flip[...], qkv[half, :, cols])
            target[size.first_qkv + part] = grad.astype(BF16).reshape(SHARDS, ROWS, LANES)
        if half == 1:
            send_pairs(size.first_qkv, size.pieces - size.first_qkv)
    for half in range(2):
        table = vec if half == 0 else vec_other
        table[6:7, 0:local] = matmul(ones, qkv[half, :, 0:local])[0:1]
        table[6:7, local : 2 * local] = matmul(ones, qkv[half, :, 2 * local : 3 * local])[0:1]
    hidden[...] = matmul_right(qkv[0], wqkv[0])
    hidden[...] += matmul_right(qkv[1], wqkv[1])

    def first_back(tile, carry):
        sum_gain, sum_shift = carry
        rows = pl.ds(pl.multiple_of(tile * tiny, tiny), tiny)
        unit, rstd = norm_parts(x_s[rows].astype(F32))
        grad = hidden[rows]
        ffn[rows] = dn2[rows] + norm_back(grad * gain_attn[...], unit, rstd)
        return sum_gain + fold(grad * unit), sum_shift + fold(grad)

    sum_gain, sum_shift = lax.fori_loop(0, SEQ // tiny, first_back, (zero, zero))
    both(2, jnp.sum(sum_gain, axis=0, keepdims=True))
    both(3, jnp.sum(sum_shift, axis=0, keepdims=True))
    grad_copies = row_copies(ffn, out_grad, 1)
    for item in grad_copies:
        item.start()

    def vector_copy(step):
        if step == 0:
            source, partner = vec_other, {"tensor": 1 - core}
        else:
            bit = lax.rem(lax.div(me, 1 << (step - 1)), 2)
            source, partner = vec, {"dp": me + (1 - 2 * bit) * (1 << (step - 1))}
        return pltpu.make_async_remote_copy(
            src_ref=source,
            dst_ref=vec_landed.at[step],
            send_sem=vec_send.at[step],
            recv_sem=vec_recv.at[step],
            device_id=partner,
            device_id_type=MESH,
        )

    for step in range(bits + 1):
        vector_copy(step).start()
        ticks(time, 1)
        time += 1
        vector_copy(step).wait()
        vec[...] += vec_landed[step]
    vector_store = pltpu.make_async_copy(vec, out_vectors, row_sem.at[2])
    vector_store.start()
    ticks(time, pieces + LAG * sends - time)

    def finish(piece, carry):
        pair_copy(piece).wait_send()
        for step in range(bits, sends):
            copy(piece, step).wait_send()
        store(piece).wait()
        return carry

    lax.fori_loop(0, pieces, finish, 0)
    for item in gathers:
        item.wait_send()
    for local_copy, remote_copy in (result_copies, grad_copies):
        local_copy.wait()
        remote_copy.wait()
    vector_store.wait()


def run_layer(size, arrays, vectors):
    width, local, hidden = size.width, size.local, size.hidden
    rows = arrays[0].shape[0]
    steps = size.sends
    rank = pltpu.SemaphoreType
    any_space = pl.BlockSpec(memory_space=pl.ANY)
    in_vmem = pl.BlockSpec(memory_space=pltpu.VMEM)
    piece_shape = (size.pieces, SHARDS, ROWS, LANES)
    scratch = [
        pltpu.VMEM((2, width, 3 * local), BF16),
        pltpu.VMEM((2 * local, width), BF16),
        pltpu.VMEM((2, width, hidden), BF16),
        pltpu.VMEM((2, hidden, width), BF16),
        pltpu.VMEM((1, local), F32),
        pltpu.VMEM((1, local), F32),
        pltpu.VMEM((1, hidden), F32),
        pltpu.VMEM((SEQ, width), BF16),
        pltpu.VMEM((SEQ, width), BF16),
        pltpu.VMEM((SEQ, width), BF16),
        pltpu.VMEM((2, SEQ, 3 * local), BF16),
        pltpu.VMEM((SEQ, width), BF16),
        pltpu.VMEM((2 * local // HEAD, 1, SEQ), F32),
        pltpu.VMEM((SEQ, width), F32),
        pltpu.VMEM((SEQ, width), BF16),
        pltpu.VMEM((width, SEQ), BF16),
        pltpu.VMEM((SEQ, width), F32),
        pltpu.VMEM((SEQ, width), F32),
        pltpu.VMEM((SEQ, width), BF16),
        pltpu.VMEM((SEQ, width), BF16),
        pltpu.VMEM((width, SEQ), BF16),
        pltpu.VMEM((256, width), F32),
        pltpu.VMEM((256, width), F32),
        pltpu.VMEM((SEQ, width), BF16),
        pltpu.VMEM((SEQ, width), BF16),
        pltpu.VMEM((SEQ, width), BF16),
        pltpu.VMEM((LANES // HEAD, SEQ, SEQ), BF16),
        pltpu.VMEM((LANES // HEAD, SEQ, SEQ), BF16),
        pltpu.VMEM(piece_shape, BF16),
        pltpu.VMEM(piece_shape, BF16),
        pltpu.VMEM(piece_shape, BF16),
        pltpu.VMEM((size.pieces, size.landing, ROWS, LANES), BF16),
        pltpu.VMEM((16, width), F32),
        pltpu.VMEM((16, width), F32),
        pltpu.VMEM((size.bits + 1, 16, width), F32),
        rank.DMA((8,)),
        rank.DMA((9,)),
        rank.DMA((9,)),
        rank.DMA((size.pieces,)),
        rank.DMA((size.pieces,)),
        rank.DMA((size.pieces, steps)),
        rank.DMA((size.pieces, steps)),
        rank.REGULAR((size.pieces, size.halving)),
        rank.DMA((size.pieces,)),
        rank.DMA((size.bits + 1,)),
        rank.DMA((size.bits + 1,)),
        rank.DMA((2,)),
        rank.DMA((2,)),
        rank.DMA((3,)),
    ]
    return pl.pallas_call(
        functools.partial(layer_kernel, size),
        out_shape=(
            jax.ShapeDtypeStruct((rows, width), BF16),
            jax.ShapeDtypeStruct((rows, width), F32),
            jax.ShapeDtypeStruct(piece_shape, BF16),
            jax.ShapeDtypeStruct((16, width), F32),
        ),
        in_specs=[any_space] * len(arrays) + [in_vmem] * len(vectors),
        out_specs=(any_space,) * 4,
        scratch_shapes=scratch,
        compiler_params=pltpu.CompilerParams(
            collective_id=0, has_side_effects=True, vmem_limit_bytes=67043328
        ),
        name="layer",
    )(*arrays, *vectors)


def unpack_kernel(size, pieces, vectors, *refs):
    g_wq, g_wk, g_wv, g_wo, g_wi, g_wb = refs[:6]
    rows_out = refs[6:15]
    held, s_in, s_back, s_qkv, s_out, sem, out_sem = refs[15:]
    width, local = size.width, size.local
    wide = 2 * LANES
    half_rows = ROWS * SHARDS // 2
    spans = []
    for chunk in range(size.chunks):
        first = chunk * size.per_chunk
        spans.append((first, size.block))
        spans.append((first + size.block, size.block))
    spans.append((size.first_out, size.first_qkv - size.first_out))
    for index in range(3):
        spans.append((size.first_qkv + index * local // LANES, local // LANES))
    copies = []
    for index, (first, amount) in enumerate(spans):
        item = pltpu.make_async_copy(
            pieces.at[pl.ds(first, amount)], held.at[pl.ds(first, amount)], sem.at[index]
        )
        item.start()
        copies.append(item)
    for ref, row, begin, amount in zip(
        rows_out,
        (6, 6, 0, 7, 1, 2, 3, 4, 5),
        (0, local, 0, 0, 0, 0, 0, 0, 0),
        (local, local, width, width, width, width, width, width, width),
    ):
        for chunk in range(ref.shape[1] // amount):
            ref[:, chunk * amount : (chunk + 1) * amount] = vectors[
                row + chunk : row + chunk + 1, begin : begin + amount
            ]

    outs = []

    def put(source, target):
        item = pltpu.make_async_copy(source, target, out_sem.at[len(outs)])
        item.start()
        outs.append(item)

    def columns(first, amount, target, begin):
        for index in range(amount):
            target[:, begin + index * LANES : begin + (index + 1) * LANES] = (
                held[first + index].reshape(SHARDS * ROWS, LANES).astype(F32)
            )

    def blocks(first, rows, target, begin):
        for block in range(rows // half_rows):
            for part in range(width // wide):
                for side in range(2):
                    value = held[
                        first + block * (width // wide) + part,
                        side * (SHARDS // 2) : (side + 1) * (SHARDS // 2),
                    ]
                    target[
                        begin + block * half_rows : begin + (block + 1) * half_rows,
                        part * wide + side * LANES : part * wide + (side + 1) * LANES,
                    ] = value.reshape(half_rows, LANES).astype(F32)

    at = 0
    for chunk in range(size.chunks):
        first = chunk * size.per_chunk
        copies[at].wait()
        columns(first, size.block, s_in.at[chunk], 0)
        put(s_in.at[chunk], g_wi.at[:, pl.ds(chunk * width, width)])
        copies[at + 1].wait()
        blocks(first + size.block, width, s_back, chunk * width)
        put(
            s_back.at[pl.ds(chunk * width, width)],
            g_wb.at[pl.ds(chunk * width, width)],
        )
        at += 2
    copies[at].wait()
    blocks(size.first_out, local, s_out, 0)
    put(s_out, g_wo)
    at += 1
    for index, target in enumerate((g_wq, g_wk, g_wv)):
        copies[at].wait()
        columns(size.first_qkv + index * local // LANES, local // LANES, s_qkv.at[index], 0)
        put(s_qkv.at[index], target)
        at += 1
    for item in outs:
        item.wait()


def unpack(size, pieces, vectors):
    width, local, hidden = size.width, size.local, size.hidden
    any_space = pl.BlockSpec(memory_space=pl.ANY)
    in_vmem = pl.BlockSpec(memory_space=pltpu.VMEM)
    matrices = [(width, local)] * 3 + [(local, width), (width, hidden), (hidden, width)]
    rows = [local, local, width, hidden, width, width, width, width, width]
    transfers = 2 * size.chunks + 4
    return pl.pallas_call(
        functools.partial(unpack_kernel, size),
        out_shape=tuple(jax.ShapeDtypeStruct(shape, F32) for shape in matrices)
        + tuple(jax.ShapeDtypeStruct((1, amount), F32) for amount in rows),
        in_specs=[any_space, in_vmem],
        out_specs=(any_space,) * 6 + (in_vmem,) * 9,
        scratch_shapes=[
            pltpu.VMEM(pieces.shape, BF16),
            pltpu.VMEM((size.chunks, width, width), F32),
            pltpu.VMEM((hidden, width), F32),
            pltpu.VMEM((3, width, local), F32),
            pltpu.VMEM((local, width), F32),
            pltpu.SemaphoreType.DMA((transfers,)),
            pltpu.SemaphoreType.DMA((transfers,)),
        ],
        compiler_params=pltpu.CompilerParams(vmem_limit_bytes=48 << 20),
        name="unpack",
    )(pieces, vectors)


def on_device(
    tokens,
    cotangent,
    w_query,
    b_query,
    w_key,
    w_value,
    b_value,
    w_out,
    b_out,
    w_in,
    b_in,
    w_back,
    b_back,
    gain_attn,
    shift_attn,
    gain_ffn,
    shift_ffn,
):
    size = Sizes(lax.axis_size("dp"), tokens, w_query, w_in)
    assert tokens.shape[0] == SEQ * lax.axis_size("tensor") and lax.axis_size("tensor") == 2
    assert size.count == 1 << size.bits and size.width == SHARDS * ROWS
    vectors = (
        b_query,
        b_value,
        b_out,
        b_in,
        b_back,
        gain_attn,
        shift_attn,
        gain_ffn,
        shift_ffn,
    )
    rows, grad_rows, pieces, sums = run_layer(
        size,
        (tokens, cotangent, w_query, w_key, w_value, w_out, w_in, w_back),
        tuple(item.reshape(1, -1) for item in vectors),
    )
    outs = unpack(size, pieces, sums)
    g_wq, g_wk, g_wv, g_wo, g_wi, g_wb = outs[:6]
    g_bq, g_bv, g_bo, g_bi, g_bb, g_ga, g_sa, g_gf, g_sf = (item.reshape(-1) for item in outs[6:])
    return (
        rows,
        grad_rows,
        g_wq,
        g_bq,
        g_wk,
        g_wv,
        g_bv,
        g_wo,
        g_bo,
        g_wi,
        g_bi,
        g_wb,
        g_bb,
        g_ga,
        g_sa,
        g_gf,
        g_sf,
    )


def solution(mesh):
    columns, rows, vector, whole = P(None, "tensor"), P("tensor", None), P("tensor"), P()
    weights = (
        columns,
        vector,
        columns,
        columns,
        vector,
        rows,
        whole,
        columns,
        vector,
        rows,
        whole,
        whole,
        whole,
        whole,
        whole,
    )
    data = (P("dp", None), P("dp", None))
    return jax.shard_map(
        on_device, mesh=mesh, in_specs=data + weights, out_specs=data + weights, check_vma=False
    )
```

```python
import functools

import jax
import jax.numpy as jnp
from jax import lax
from jax.experimental import pallas as pl
from jax.experimental.pallas import tpu as pltpu
from jax.sharding import PartitionSpec as P

HEAD = 64
SEQ = 512
EPS = 1e-12
SHARDS = 16
ROWS = 48
LANES = 128
LAG = 2
DELAY = 0
MESH = pl.DeviceIdType.MESH
F32 = jnp.float32
BF16 = jnp.bfloat16


def matmul(left, right):
    return jnp.dot(left, right, preferred_element_type=F32)


def matmul_left(left, right):
    return lax.dot_general(left, right, (((0,), (0,)), ((), ())), preferred_element_type=F32)


def matmul_right(left, right):
    return lax.dot_general(left, right, (((1,), (1,)), ((), ())), preferred_element_type=F32)


def norm_parts(value):
    mean = jnp.mean(value, axis=-1, keepdims=True)
    centred = value - mean
    rstd = lax.rsqrt(jnp.mean(centred * centred, axis=-1, keepdims=True) + EPS)
    return centred * rstd, rstd


def norm_back(scaled, unit, rstd):
    return rstd * (
        scaled
        - jnp.mean(scaled, axis=-1, keepdims=True)
        - unit * jnp.mean(scaled * unit, axis=-1, keepdims=True)
    )


def row_of(ref):
    return ref[...].reshape(1, -1)


def fold(value):
    return jnp.sum(value.reshape(value.shape[0] // 8, 8, value.shape[1]), axis=0)


class Sizes:
    def __init__(self, count, tokens, w_query, w_in):
        self.count = count
        self.bits = count.bit_length() - 1
        self.halving = min(self.bits, SHARDS.bit_length() - 1)
        self.sends = self.bits + self.halving
        self.width = tokens.shape[1]
        self.local = w_query.shape[1]
        self.hidden = w_in.shape[1]
        self.chunks = self.hidden // self.width
        self.block = self.width // LANES
        self.per_chunk = 2 * self.block
        self.first_out = self.chunks * self.per_chunk
        self.first_qkv = self.first_out + self.local // LANES
        self.pieces = self.first_qkv + 3 * self.local // LANES
        self.landing = SHARDS - (SHARDS >> self.halving) + self.bits - self.halving


def bit_orders(bits, halving):
    low = list(range(halving))
    high = list(range(halving, bits))
    if halving < 3:
        return [low + high] * 3
    return [low + high, [1, 0] + low[2:] + high, low[2:] + low[:2] + high]


def layer_kernel(
    size,
    tokens,
    cotangent,
    w_query,
    w_key,
    w_value,
    w_out,
    w_in,
    w_back,
    b_query,
    b_value,
    b_out,
    b_in,
    b_back,
    gain_attn,
    shift_attn,
    gain_ffn,
    shift_ffn,
    out_rows,
    out_grad,
    out_pieces,
    out_vectors,
    wqkv,
    wo,
    wi,
    wb,
    bias_q,
    bias_v,
    bias_i,
    x_s,
    dy_s,
    normed,
    qkv,
    mixed,
    lse,
    hidden,
    normed2,
    flip2,
    ffn,
    dn2,
    act,
    dpre,
    flip,
    wide_a,
    wide_b,
    dattn,
    dmixed,
    result,
    probs_t,
    dscores_t,
    held,
    other,
    pair,
    landed,
    vec,
    vec_other,
    vec_landed,
    load_sem,
    weight_send,
    weight_recv,
    pair_send,
    pair_recv,
    send_sem,
    recv_sem,
    store_sem,
    vec_send,
    vec_recv,
    row_send,
    row_recv,
    row_sem,
):
    me = lax.axis_index("dp")
    core = lax.axis_index("tensor")
    width, local = size.width, size.local
    bits, halving, sends, pieces = size.bits, size.halving, size.sends, size.pieces
    orders = bit_orders(bits, halving)
    my_rows = pl.ds(pl.multiple_of(core * SEQ, SEQ), SEQ)

    def colour_of(piece):
        place = lax.rem(piece, 13)
        third = (place == 4) | (place == 8) | (place == 12)
        return jnp.where(third, 2, lax.rem(place, 2))

    def bit_at(colour, level):
        strides = [1 << order[level] for order in orders]
        stride = jnp.where(
            colour == 0, strides[0], jnp.where(colour == 1, strides[1], strides[2])
        )
        return stride, lax.rem(lax.div(me, stride), 2)

    def base_of(colour, level):
        base = 0
        for earlier in range(min(level, halving)):
            base = base + bit_at(colour, earlier)[1] * (SHARDS >> (earlier + 1))
        return base

    def landing_of(level):
        if level < halving:
            return SHARDS - (SHARDS >> level), SHARDS >> (level + 1)
        return SHARDS - (SHARDS >> halving) + level - halving, SHARDS >> halving

    def level_of(step):
        return step if step < bits else sends - 1 - step

    def copy(piece, step):
        colour = colour_of(piece)
        level = level_of(step)
        stride, bit = bit_at(colour, level)
        base = base_of(colour, level)
        if level < halving:
            half = SHARDS >> (level + 1)
            start = base + ((1 - bit) if step < bits else bit) * half
        else:
            half = SHARDS >> halving
            start = base
        if step < bits:
            source = held.at[piece, pl.ds(start, half)]
            target = landed.at[piece, pl.ds(landing_of(level)[0], half)]
        else:
            source = pair.at[piece, pl.ds(start, half)]
            target = source
        return pltpu.make_async_remote_copy(
            src_ref=source,
            dst_ref=target,
            send_sem=send_sem.at[piece, step],
            recv_sem=recv_sem.at[piece, step],
            device_id={"dp": me + (1 - 2 * bit) * stride},
            device_id_type=MESH,
        )

    def add_level(piece, level):
        colour = colour_of(piece)
        base = base_of(colour, level + 1)
        place, half = landing_of(level)
        total = held if level < bits - 1 else pair
        group = min(half, 4)

        def some(index, carry):
            mine = held[piece, pl.ds(base + index * group, group)]
            theirs = landed[piece, pl.ds(place + index * group, group)]
            total[piece, pl.ds(base + index * group, group)] = mine + theirs
            return carry

        lax.fori_loop(0, half // group, some, 0)

    def pair_copy(piece):
        return pltpu.make_async_remote_copy(
            src_ref=other.at[piece],
            dst_ref=pair.at[piece],
            send_sem=pair_send.at[piece],
            recv_sem=pair_recv.at[piece],
            device_id={"tensor": 1 - core},
            device_id_type=MESH,
        )

    def store(piece):
        return pltpu.make_async_copy(pair.at[piece], out_pieces.at[piece], store_sem.at[piece])

    def advance(piece, step):
        if step == 0:
            pair_copy(piece).wait_recv()

            def some(index, carry):
                shards = pl.ds(index * 4, 4)
                held[piece, shards] = held[piece, shards] + pair[piece, shards]
                return carry

            lax.fori_loop(0, SHARDS // 4, some, 0)
        else:
            copy(piece, step - 1).wait_recv()
            if halving < step <= bits:
                copy(piece, step - 1).wait_send()
            if step <= bits:
                add_level(piece, step - 1)
        if step < sends:
            copy(piece, step).start()
        else:
            store(piece).start()
            for earlier in early_sends:
                copy(piece, earlier).wait_send()

    early_sends = range(halving)

    def offset_of(step):
        return LAG * step + (DELAY if step >= bits else 0)

    def tick(time, carry):
        for step in range(sends + 1):
            piece = time - offset_of(step)

            @pl.when((piece >= 0) & (piece < pieces))
            def _():
                advance(piece, step)

        return carry

    def ticks(first, amount):
        lax.fori_loop(first, first + amount, tick, 0)

    def send_pairs(first, amount):
        def one(piece, carry):
            pair_copy(piece).start()
            return carry

        lax.fori_loop(first, first + amount, one, 0)

    def load(source, target, place):
        return pltpu.make_async_copy(source, target, load_sem.at[place])

    loads = [
        load(tokens.at[my_rows], x_s, 0),
        load(cotangent.at[my_rows], dy_s, 1),
        load(w_query, wqkv.at[0, :, pl.ds(0, local)], 2),
        load(w_key, wqkv.at[0, :, pl.ds(local, local)], 3),
        load(w_value, wqkv.at[0, :, pl.ds(2 * local, local)], 4),
        load(w_out, wo.at[pl.ds(0, local)], 5),
        load(w_in, wi.at[0], 6),
        load(w_back, wb.at[0], 7),
    ]
    for item in loads:
        item.start()

    barrier = pltpu.get_barrier_semaphore()
    pl.semaphore_signal(barrier, inc=1, device_id={"tensor": 1 - core}, device_id_type=MESH)
    for bit in range(bits):
        mine = lax.rem(lax.div(me, 1 << bit), 2)
        pl.semaphore_signal(
            barrier,
            inc=1,
            device_id={"dp": me + (1 - 2 * mine) * (1 << bit)},
            device_id_type=MESH,
        )
    pl.semaphore_wait(barrier, bits + 1)

    def to_partner(source, target, place):
        return pltpu.make_async_remote_copy(
            src_ref=source,
            dst_ref=target,
            send_sem=weight_send.at[place],
            recv_sem=weight_recv.at[place],
            device_id={"tensor": 1 - core},
            device_id_type=MESH,
        )

    gathers = [
        to_partner(b_query, bias_q, 0),
        to_partner(b_value, bias_v, 1),
        to_partner(b_in, bias_i, 2),
        to_partner(w_query, wqkv.at[1, :, pl.ds(0, local)], 3),
        to_partner(w_key, wqkv.at[1, :, pl.ds(local, local)], 4),
        to_partner(w_value, wqkv.at[1, :, pl.ds(2 * local, local)], 5),
        to_partner(w_out, wo.at[pl.ds(local, local)], 6),
        to_partner(w_in, wi.at[1], 7),
        to_partner(w_back, wb.at[1], 8),
    ]
    for item in gathers:
        item.start()

    vec[...] = jnp.zeros_like(vec)
    vec_other[...] = jnp.zeros_like(vec_other)
    ffn[...] = jnp.zeros_like(ffn)
    dn2[...] = jnp.zeros_like(dn2)

    small = 128
    loads[0].wait()

    def first_norm(tile, carry):
        rows = pl.ds(pl.multiple_of(tile * small, small), small)
        unit, rstd = norm_parts(x_s[rows].astype(F32))
        normed[rows] = (unit * row_of(gain_attn) + row_of(shift_attn)).astype(BF16)
        return carry

    lax.fori_loop(0, SEQ // small, first_norm, 0)

    for half in range(2):
        if half == 0:
            for item in loads[2:5]:
                item.wait()
            bias_query, bias_value = b_query, b_value
        else:
            for item in gathers[0:2] + gathers[3:6]:
                item.wait_recv()
            bias_query, bias_value = bias_q, bias_v
        qkv[half, :, 0:local] = (
            matmul(normed[...], wqkv[half, :, 0:local]) + row_of(bias_query)
        ).astype(BF16)
        qkv[half, :, local : 2 * local] = matmul(
            normed[...], wqkv[half, :, local : 2 * local]
        ).astype(BF16)
        qkv[half, :, 2 * local : 3 * local] = (
            matmul(normed[...], wqkv[half, :, 2 * local : 3 * local]) + row_of(bias_value)
        ).astype(BF16)

    pairs_half = local // LANES
    scale = HEAD ** (-0.5)
    lane = lax.broadcasted_iota(jnp.int32, (1, LANES), 1)
    masks = [
        jnp.where((lane >= part * HEAD) & (lane < (part + 1) * HEAD), 1.0, 0.0).astype(BF16)
        for part in range(LANES // HEAD)
    ]
    queries = 128

    def columns(index, group):
        return pl.ds(pl.multiple_of(group * local + index * LANES, LANES), LANES)

    def attend(index, carry):
        half, place = lax.div(index, pairs_half), lax.rem(index, pairs_half)
        key = qkv[half, :, columns(place, 1)]
        value = qkv[half, :, columns(place, 2)]
        total = None
        for part, mask in enumerate(masks):
            for tile in range(SEQ // queries):
                rows = slice(tile * queries, (tile + 1) * queries)
                query = qkv[half, rows, columns(place, 0)] * (mask * scale).astype(BF16)
                scores = matmul_right(key, query)
                top = jnp.max(scores, axis=0, keepdims=True)
                expo = jnp.exp(scores - top)
                amount = jnp.sum(expo, axis=0, keepdims=True)
                lse[index * 2 + part, :, rows] = top + jnp.log(amount)
                probs_t[part, :, rows] = (expo * (1.0 / amount)).astype(BF16)
            term = matmul_left(probs_t[part], value * mask)
            total = term if total is None else total + term
        mixed[:, pl.ds(pl.multiple_of(index * LANES, LANES), LANES)] = total.astype(BF16)
        return carry

    lax.fori_loop(0, 2 * pairs_half, attend, 0)

    loads[5].wait()
    gathers[6].wait_recv()
    hidden[...] = matmul(mixed[...], wo[...])

    def second_norm(tile, carry):
        rows = pl.ds(pl.multiple_of(tile * small, small), small)
        whole = x_s[rows].astype(F32) + (hidden[rows] + row_of(b_out))
        hidden[rows] = whole
        unit, rstd = norm_parts(whole)
        normed2[rows] = (unit * row_of(gain_ffn) + row_of(shift_ffn)).astype(BF16)
        return carry

    lax.fori_loop(0, SEQ // small, second_norm, 0)
    flip2[...] = normed2[...].T

    loads[1].wait()
    loads[6].wait()
    loads[7].wait()
    gathers[2].wait_recv()
    gathers[7].wait_recv()
    gathers[8].wait_recv()
    ones = jnp.ones((16, SEQ), BF16)
    fine = 32
    tall = 256

    def hand_in(target, first, grad, kind, part):
        wide = 2 * LANES
        if kind == "in":
            for side in range(2):
                target[first + 2 * part + side] = (
                    grad[:, side * LANES : (side + 1) * LANES]
                    .astype(BF16)
                    .reshape(SHARDS, ROWS, LANES)
                )
        else:
            blocks = grad.shape[0] // (ROWS * SHARDS // 2)
            for block in range(blocks):
                rows = slice(block * ROWS * SHARDS // 2, (block + 1) * ROWS * SHARDS // 2)
                for side in range(2):
                    target[
                        first + (width // wide) * block + part,
                        side * (SHARDS // 2) : (side + 1) * (SHARDS // 2),
                    ] = (
                        grad[rows, side * LANES : (side + 1) * LANES]
                        .astype(BF16)
                        .reshape(SHARDS // 2, ROWS, LANES)
                    )

    def feed(chunk, half, slots):
        begin = pl.multiple_of(chunk * width, width)
        units = pl.ds(begin, width)
        bias_row = b_in if half == 0 else bias_i
        target = held if half == 0 else other
        first = chunk * size.per_chunk

        def rows_tile(tile, carry):
            rows = pl.ds(pl.multiple_of(tile * tall, tall), tall)
            wide_a[...] = matmul(normed2[rows], wi[half, :, units])
            wide_b[...] = matmul_right(dy_s[rows], wb[half, units, :])

            def inner(step, carry):
                piece = pl.ds(pl.multiple_of(step * fine, fine), fine)
                there = pl.ds(pl.multiple_of(tile * tall + step * fine, fine), fine)
                pre = wide_a[piece] + bias_row[units].reshape(1, -1)
                phi = 0.5 * (1.0 + lax.erf(pre * 0.7071067811865476))
                act[there] = (pre * phi).astype(BF16)
                slope = phi + pre * jnp.exp(-0.5 * pre * pre) * 0.3989422804014327
                dpre[there] = (wide_b[piece] * slope).astype(BF16)
                return carry

            lax.fori_loop(0, tall // fine, inner, 0)
            return carry

        lax.fori_loop(0, SEQ // tall, rows_tile, 0)
        flip[...] = act[...].T
        slots(0)
        for part in range(width // 256):
            cols = slice(part * 256, (part + 1) * 256)
            hand_in(target, first, matmul(flip2[...], dpre[:, cols]), "in", part)
        for part in range(width // 256):
            cols = slice(part * 256, (part + 1) * 256)
            hand_in(target, first + size.block, matmul(flip[...], dy_s[:, cols]), "out", part)
        slots(1)
        ffn[...] += matmul(act[...], wb[half, units, :])
        dn2[...] += matmul_right(dpre[...], wi[half, :, units])
        sums = matmul(ones, dpre[...])[0:1]
        (vec if half == 0 else vec_other)[pl.ds(7 + chunk, 1)] = sums

    def feed_both(chunk, carry):
        def slots(offset, half):
            def place(index):
                if index == 0:
                    first = 1 + (chunk - 1) * 4 + offset
                    lax.fori_loop(first, jnp.where(chunk > 0, first + 1, first), tick, 0)
                elif half == 1:
                    send_pairs(chunk * size.per_chunk, size.per_chunk)
                    first = 2 + (chunk - 1) * 4
                    lax.fori_loop(first, jnp.where(chunk > 0, first + 1, first), tick, 0)
                else:
                    ticks(chunk * 4, 1)

            return place

        feed(chunk, 1, slots(0, 1))
        feed(chunk, 0, slots(2, 0))
        return carry

    lax.fori_loop(0, size.chunks, feed_both, 0)
    time = 4 * size.chunks - 3

    tiny = 64

    def second_back(tile, carry):
        sum_gain, sum_shift, sum_out = carry
        rows = pl.ds(pl.multiple_of(tile * tiny, tiny), tiny)
        whole = hidden[rows]
        result[rows] = (whole + (ffn[rows] + row_of(b_back))).astype(BF16)
        unit, rstd = norm_parts(whole)
        grad = dn2[rows]
        dhidden = dy_s[rows].astype(F32) + norm_back(grad * row_of(gain_ffn), unit, rstd)
        dn2[rows] = dhidden
        rounded = dhidden.astype(BF16)
        dattn[rows] = rounded
        return (
            sum_gain + fold(grad * unit),
            sum_shift + fold(grad),
            sum_out + fold(rounded.astype(F32)),
        )

    zero = jnp.zeros((8, width), F32)
    sum_gain, sum_shift, sum_out = lax.fori_loop(
        0, SEQ // tiny, second_back, (zero, zero, zero)
    )

    def both(row, value):
        vec[row : row + 1] = value
        vec_other[row : row + 1] = value

    both(0, jnp.sum(sum_out, axis=0, keepdims=True))
    both(1, matmul(ones, dy_s[...])[0:1])
    both(4, jnp.sum(sum_gain, axis=0, keepdims=True))
    both(5, jnp.sum(sum_shift, axis=0, keepdims=True))

    def row_copies(source, target, place):
        return (
            pltpu.make_async_copy(source, target.at[my_rows], row_sem.at[place]),
            pltpu.make_async_remote_copy(
                src_ref=source,
                dst_ref=target.at[my_rows],
                send_sem=row_send.at[place],
                recv_sem=row_recv.at[place],
                device_id={"tensor": 1 - core},
                device_id_type=MESH,
            ),
        )

    result_copies = row_copies(result, out_rows, 0)
    for item in result_copies:
        item.start()
    ticks(time, 1)
    time += 1

    flip[...] = mixed[...].T
    for part in range(width // 256):
        cols = slice(part * 256, (part + 1) * 256)
        grad = matmul(flip[...], dattn[:, cols])
        hand_in(held, size.first_out, grad[0:local], "out", part)
        hand_in(other, size.first_out, grad[local:], "out", part)
    send_pairs(size.first_out, size.first_qkv - size.first_out)
    dmixed[...] = matmul_right(dattn[...], wo[...]).astype(BF16)
    ticks(time, 1)
    time += 1

    def attend_back(index, carry):
        half, place = lax.div(index, pairs_half), lax.rem(index, pairs_half)
        here = pl.ds(pl.multiple_of(index * LANES, LANES), LANES)
        key = qkv[half, :, columns(place, 1)]
        value = qkv[half, :, columns(place, 2)]
        dquery, dkey, dvalue = None, None, None
        for part, mask in enumerate(masks):
            for tile in range(SEQ // queries):
                rows = slice(tile * queries, (tile + 1) * queries)
                query = qkv[half, rows, columns(place, 0)] * (mask * scale).astype(BF16)
                scores = matmul_right(key, query)
                probs = jnp.exp(scores - lse[index * 2 + part, :, rows])
                dprobs = matmul_right(value, dmixed[rows, here] * mask)
                inner = jnp.sum(dprobs * probs, axis=0, keepdims=True)
                probs_t[part, :, rows] = probs.astype(BF16)
                dscores_t[part, :, rows] = (probs * (dprobs - inner)).astype(BF16)
            query = qkv[half, :, columns(place, 0)] * (mask * scale).astype(BF16)
            terms = (
                matmul_left(dscores_t[part], key * mask),
                matmul(dscores_t[part], query),
                matmul(probs_t[part], dmixed[:, here] * mask),
            )
            if dquery is None:
                dquery, dkey, dvalue = terms
            else:
                dquery, dkey, dvalue = dquery + terms[0], dkey + terms[1], dvalue + terms[2]
        qkv[half, :, columns(place, 0)] = (dquery * scale).astype(BF16)
        qkv[half, :, columns(place, 1)] = dkey.astype(BF16)
        qkv[half, :, columns(place, 2)] = dvalue.astype(BF16)
        ticks(time + index, 1)
        return carry

    lax.fori_loop(0, 2 * pairs_half, attend_back, 0)
    time += 2 * pairs_half

    flip[...] = normed[...].T
    for half in (1, 0):
        target = held if half == 0 else other
        for part in range(3 * local // LANES):
            cols = slice(part * LANES, (part + 1) * LANES)
            grad = matmul(flip[...], qkv[half, :, cols])
            target[size.first_qkv + part] = grad.astype(BF16).reshape(SHARDS, ROWS, LANES)
        if half == 1:
            send_pairs(size.first_qkv, size.pieces - size.first_qkv)
        ticks(time, 1)
        time += 1
    for half in range(2):
        table = vec if half == 0 else vec_other
        table[6:7, 0:local] = matmul(ones, qkv[half, :, 0:local])[0:1]
        table[6:7, local : 2 * local] = matmul(ones, qkv[half, :, 2 * local : 3 * local])[0:1]
    hidden[...] = matmul_right(qkv[0], wqkv[0])
    hidden[...] += matmul_right(qkv[1], wqkv[1])
    ticks(time, 1)
    time += 1

    def first_back(tile, carry):
        sum_gain, sum_shift = carry
        rows = pl.ds(pl.multiple_of(tile * tiny, tiny), tiny)
        unit, rstd = norm_parts(x_s[rows].astype(F32))
        grad = hidden[rows]
        ffn[rows] = dn2[rows] + norm_back(grad * row_of(gain_attn), unit, rstd)
        return sum_gain + fold(grad * unit), sum_shift + fold(grad)

    sum_gain, sum_shift = lax.fori_loop(0, SEQ // tiny, first_back, (zero, zero))
    both(2, jnp.sum(sum_gain, axis=0, keepdims=True))
    both(3, jnp.sum(sum_shift, axis=0, keepdims=True))
    grad_copies = row_copies(ffn, out_grad, 1)
    for item in grad_copies:
        item.start()

    def vector_copy(step):
        if step == 0:
            source, partner = vec_other, {"tensor": 1 - core}
        else:
            bit = lax.rem(lax.div(me, 1 << (step - 1)), 2)
            source, partner = vec, {"dp": me + (1 - 2 * bit) * (1 << (step - 1))}
        return pltpu.make_async_remote_copy(
            src_ref=source,
            dst_ref=vec_landed.at[step],
            send_sem=vec_send.at[step],
            recv_sem=vec_recv.at[step],
            device_id=partner,
            device_id_type=MESH,
        )

    for step in range(bits + 1):
        vector_copy(step).start()
        ticks(time, 3)
        time += 3
        vector_copy(step).wait()
        vec[...] += vec_landed[step]
    vector_store = pltpu.make_async_copy(vec, out_vectors, row_sem.at[2])
    vector_store.start()
    ticks(time, pieces + offset_of(sends) - time)

    def finish(piece, carry):
        pair_copy(piece).wait_send()
        for step in range(bits, sends):
            copy(piece, step).wait_send()
        store(piece).wait()
        return carry

    lax.fori_loop(0, pieces, finish, 0)
    for item in gathers:
        item.wait_send()
    for local_copy, remote_copy in (result_copies, grad_copies):
        local_copy.wait()
        remote_copy.wait()
    vector_store.wait()


def run_layer(size, arrays, vectors):
    width, local, hidden = size.width, size.local, size.hidden
    rows = arrays[0].shape[0]
    steps = size.sends
    rank = pltpu.SemaphoreType
    any_space = pl.BlockSpec(memory_space=pl.ANY)
    in_vmem = pl.BlockSpec(memory_space=pltpu.VMEM)
    piece_shape = (size.pieces, SHARDS, ROWS, LANES)
    scratch = [
        pltpu.VMEM((2, width, 3 * local), BF16),
        pltpu.VMEM((2 * local, width), BF16),
        pltpu.VMEM((2, width, hidden), BF16),
        pltpu.VMEM((2, hidden, width), BF16),
        pltpu.VMEM((local,), F32),
        pltpu.VMEM((local,), F32),
        pltpu.VMEM((hidden,), F32),
        pltpu.VMEM((SEQ, width), BF16),
        pltpu.VMEM((SEQ, width), BF16),
        pltpu.VMEM((SEQ, width), BF16),
        pltpu.VMEM((2, SEQ, 3 * local), BF16),
        pltpu.VMEM((SEQ, width), BF16),
        pltpu.VMEM((2 * local // HEAD, 1, SEQ), F32),
        pltpu.VMEM((SEQ, width), F32),
        pltpu.VMEM((SEQ, width), BF16),
        pltpu.VMEM((width, SEQ), BF16),
        pltpu.VMEM((SEQ, width), F32),
        pltpu.VMEM((SEQ, width), F32),
        pltpu.VMEM((SEQ, width), BF16),
        pltpu.VMEM((SEQ, width), BF16),
        pltpu.VMEM((width, SEQ), BF16),
        pltpu.VMEM((256, width), F32),
        pltpu.VMEM((256, width), F32),
        pltpu.VMEM((SEQ, width), BF16),
        pltpu.VMEM((SEQ, width), BF16),
        pltpu.VMEM((SEQ, width), BF16),
        pltpu.VMEM((LANES // HEAD, SEQ, SEQ), BF16),
        pltpu.VMEM((LANES // HEAD, SEQ, SEQ), BF16),
        pltpu.VMEM(piece_shape, BF16),
        pltpu.VMEM(piece_shape, BF16),
        pltpu.VMEM(piece_shape, BF16),
        pltpu.VMEM((size.pieces, size.landing, ROWS, LANES), BF16),
        pltpu.VMEM((16, width), F32),
        pltpu.VMEM((16, width), F32),
        pltpu.VMEM((size.bits + 1, 16, width), F32),
        rank.DMA((8,)),
        rank.DMA((9,)),
        rank.DMA((9,)),
        rank.DMA((size.pieces,)),
        rank.DMA((size.pieces,)),
        rank.DMA((size.pieces, steps)),
        rank.DMA((size.pieces, steps)),
        rank.DMA((size.pieces,)),
        rank.DMA((size.bits + 1,)),
        rank.DMA((size.bits + 1,)),
        rank.DMA((2,)),
        rank.DMA((2,)),
        rank.DMA((3,)),
    ]
    return pl.pallas_call(
        functools.partial(layer_kernel, size),
        out_shape=(
            jax.ShapeDtypeStruct((rows, width), BF16),
            jax.ShapeDtypeStruct((rows, width), F32),
            jax.ShapeDtypeStruct(piece_shape, BF16),
            jax.ShapeDtypeStruct((16, width), F32),
        ),
        in_specs=[any_space] * len(arrays) + [in_vmem] * len(vectors),
        out_specs=(any_space,) * 4,
        scratch_shapes=scratch,
        compiler_params=pltpu.CompilerParams(
            collective_id=0, has_side_effects=True, vmem_limit_bytes=67043328
        ),
        name="layer",
    )(*arrays, *vectors)


def unpack_kernel(size, pieces, vectors_in, rows_in, grad_in, *refs):
    g_wq, g_wk, g_wv, g_wo, g_wi, g_wb, rows_end, grad_end = refs[:8]
    rows_out = refs[8:17]
    held, s_in, s_back, s_qkv, s_out, vectors, rows, grad, sem, out_sem, side_sem = refs[17:]
    width, local = size.width, size.local
    wide = 2 * LANES
    half_rows = ROWS * SHARDS // 2
    spans = []
    for chunk in range(size.chunks):
        first = chunk * size.per_chunk
        spans.append((first, size.block))
        spans.append((first + size.block, size.block))
    spans.append((size.first_out, size.first_qkv - size.first_out))
    for index in range(3):
        spans.append((size.first_qkv + index * local // LANES, local // LANES))
    copies = []
    for index, (first, amount) in enumerate(spans):
        item = pltpu.make_async_copy(
            pieces.at[pl.ds(first, amount)], held.at[pl.ds(first, amount)], sem.at[index]
        )
        item.start()
        copies.append(item)
    sides = [
        pltpu.make_async_copy(source, target, side_sem.at[index])
        for index, (source, target) in enumerate(
            ((vectors_in, vectors), (rows_in, rows), (grad_in, grad))
        )
    ]
    for item in sides:
        item.start()
    sides[0].wait()
    for ref, row, begin, amount in zip(
        rows_out,
        (6, 6, 0, 7, 1, 2, 3, 4, 5),
        (0, local, 0, 0, 0, 0, 0, 0, 0),
        (local, local, width, width, width, width, width, width, width),
    ):
        for chunk in range(ref.shape[0] // amount):
            ref[chunk * amount : (chunk + 1) * amount] = vectors[
                row + chunk, begin : begin + amount
            ]

    outs = []

    def put(source, target):
        item = pltpu.make_async_copy(source, target, out_sem.at[len(outs)])
        item.start()
        outs.append(item)

    def columns(first, amount, target, begin):
        for index in range(amount):
            target[:, begin + index * LANES : begin + (index + 1) * LANES] = (
                held[first + index].reshape(SHARDS * ROWS, LANES).astype(F32)
            )

    def blocks(first, rows, target, begin):
        for block in range(rows // half_rows):
            for part in range(width // wide):
                for side in range(2):
                    value = held[
                        first + block * (width // wide) + part,
                        side * (SHARDS // 2) : (side + 1) * (SHARDS // 2),
                    ]
                    target[
                        begin + block * half_rows : begin + (block + 1) * half_rows,
                        part * wide + side * LANES : part * wide + (side + 1) * LANES,
                    ] = value.reshape(half_rows, LANES).astype(F32)

    at = 0
    for chunk in range(size.chunks):
        first = chunk * size.per_chunk
        copies[at].wait()
        columns(first, size.block, s_in.at[chunk], 0)
        put(s_in.at[chunk], g_wi.at[:, pl.ds(chunk * width, width)])
        copies[at + 1].wait()
        blocks(first + size.block, width, s_back, chunk * width)
        put(
            s_back.at[pl.ds(chunk * width, width)],
            g_wb.at[pl.ds(chunk * width, width)],
        )
        at += 2
    copies[at].wait()
    blocks(size.first_out, local, s_out, 0)
    put(s_out, g_wo)
    at += 1
    for index, target in enumerate((g_wq, g_wk, g_wv)):
        copies[at].wait()
        columns(size.first_qkv + index * local // LANES, local // LANES, s_qkv.at[index], 0)
        put(s_qkv.at[index], target)
        at += 1
    sides[1].wait()
    put(rows, rows_end)
    sides[2].wait()
    put(grad, grad_end)
    for item in outs:
        item.wait()


def unpack(size, pieces, vectors, block_rows, grad_rows):
    width, local, hidden = size.width, size.local, size.hidden
    any_space = pl.BlockSpec(memory_space=pl.ANY)
    in_vmem = pl.BlockSpec(memory_space=pltpu.VMEM)
    matrices = [(width, local)] * 3 + [(local, width), (width, hidden), (hidden, width)]
    rows = [local, local, width, hidden, width, width, width, width, width]
    transfers = 2 * size.chunks + 6
    return pl.pallas_call(
        functools.partial(unpack_kernel, size),
        out_shape=tuple(jax.ShapeDtypeStruct(shape, F32) for shape in matrices)
        + tuple(jax.ShapeDtypeStruct(item.shape, item.dtype) for item in (block_rows, grad_rows))
        + tuple(jax.ShapeDtypeStruct((amount,), F32) for amount in rows),
        in_specs=[any_space] * 4,
        out_specs=(any_space,) * 8 + (in_vmem,) * 9,
        scratch_shapes=[
            pltpu.VMEM(pieces.shape, BF16),
            pltpu.VMEM((size.chunks, width, width), F32),
            pltpu.VMEM((hidden, width), F32),
            pltpu.VMEM((3, width, local), F32),
            pltpu.VMEM((local, width), F32),
            pltpu.VMEM(vectors.shape, F32),
            pltpu.VMEM(block_rows.shape, BF16),
            pltpu.VMEM(grad_rows.shape, F32),
            pltpu.SemaphoreType.DMA((transfers,)),
            pltpu.SemaphoreType.DMA((transfers,)),
            pltpu.SemaphoreType.DMA((3,)),
        ],
        compiler_params=pltpu.CompilerParams(vmem_limit_bytes=48 << 20),
        name="unpack",
    )(pieces, vectors, block_rows, grad_rows)


def on_device(
    tokens,
    cotangent,
    w_query,
    b_query,
    w_key,
    w_value,
    b_value,
    w_out,
    b_out,
    w_in,
    b_in,
    w_back,
    b_back,
    gain_attn,
    shift_attn,
    gain_ffn,
    shift_ffn,
):
    size = Sizes(lax.axis_size("dp"), tokens, w_query, w_in)
    assert tokens.shape[0] == SEQ * lax.axis_size("tensor") and lax.axis_size("tensor") == 2
    assert size.count == 1 << size.bits and size.width == SHARDS * ROWS
    vectors = (
        b_query,
        b_value,
        b_out,
        b_in,
        b_back,
        gain_attn,
        shift_attn,
        gain_ffn,
        shift_ffn,
    )
    rows, grad_rows, pieces, sums = run_layer(
        size,
        (tokens, cotangent, w_query, w_key, w_value, w_out, w_in, w_back),
        vectors,
    )
    outs = unpack(size, pieces, sums, rows, grad_rows)
    g_wq, g_wk, g_wv, g_wo, g_wi, g_wb = outs[:6]
    g_bq, g_bv, g_bo, g_bi, g_bb, g_ga, g_sa, g_gf, g_sf = outs[8:]
    return (
        *outs[6:8],
        g_wq,
        g_bq,
        g_wk,
        g_wv,
        g_bv,
        g_wo,
        g_bo,
        g_wi,
        g_bi,
        g_wb,
        g_bb,
        g_ga,
        g_sa,
        g_gf,
        g_sf,
    )


def solution(mesh):
    columns, rows, vector, whole = P(None, "tensor"), P("tensor", None), P("tensor"), P()
    weights = (
        columns,
        vector,
        columns,
        columns,
        vector,
        rows,
        whole,
        columns,
        vector,
        rows,
        whole,
        whole,
        whole,
        whole,
        whole,
    )
    data = (P("dp", None), P("dp", None))
    return jax.shard_map(
        on_device, mesh=mesh, in_specs=data + weights, out_specs=data + weights, check_vma=False
    )
```

```python
import functools

import jax
import jax.numpy as jnp
from jax import lax
from jax.experimental import pallas as pl
from jax.experimental.pallas import tpu as pltpu
from jax.sharding import PartitionSpec as P

HEAD = 64
SEQ = 512
EPS = 1e-12
SHARDS = 16
ROWS = 48
LANES = 128
LAG = 4
HEAD_START = 2
EACH = 2
NORM_TICKS = 2
OUT_TICKS = 2
PAIR_TICKS = 2
QKV_TICKS = 2
DELAY = 0
MESH = pl.DeviceIdType.MESH
F32 = jnp.float32
BF16 = jnp.bfloat16


def matmul(left, right):
    return jnp.dot(left, right, preferred_element_type=F32)


def matmul_left(left, right):
    return lax.dot_general(left, right, (((0,), (0,)), ((), ())), preferred_element_type=F32)


def matmul_right(left, right):
    return lax.dot_general(left, right, (((1,), (1,)), ((), ())), preferred_element_type=F32)


def norm_parts(value):
    mean = jnp.mean(value, axis=-1, keepdims=True)
    centred = value - mean
    rstd = lax.rsqrt(jnp.mean(centred * centred, axis=-1, keepdims=True) + EPS)
    return centred * rstd, rstd


def norm_back(scaled, unit, rstd):
    return rstd * (
        scaled
        - jnp.mean(scaled, axis=-1, keepdims=True)
        - unit * jnp.mean(scaled * unit, axis=-1, keepdims=True)
    )


def row_of(ref):
    return ref[...].reshape(1, -1)


def fold(value):
    return jnp.sum(value.reshape(value.shape[0] // 8, 8, value.shape[1]), axis=0)


class Sizes:
    def __init__(self, count, tokens, w_query, w_in):
        self.count = count
        self.bits = count.bit_length() - 1
        self.halving = min(self.bits, SHARDS.bit_length() - 1)
        self.sends = self.bits + self.halving
        self.width = tokens.shape[1]
        self.local = w_query.shape[1]
        self.hidden = w_in.shape[1]
        self.chunks = self.hidden // self.width
        self.block = self.width // LANES
        self.per_chunk = 2 * self.block
        self.first_out = self.chunks * self.per_chunk
        self.first_qkv = self.first_out + self.local // LANES
        self.pieces = self.first_qkv + 3 * self.local // LANES
        self.landing = SHARDS - (SHARDS >> self.halving) + self.bits - self.halving


def bit_orders(bits, halving):
    low = list(range(halving))
    high = list(range(halving, bits))
    if halving < 3:
        return [low + high] * 3
    return [low + high, [1, 0] + low[2:] + high, low[2:] + low[:2] + high]


def layer_kernel(
    size,
    tokens,
    cotangent,
    w_query,
    w_key,
    w_value,
    w_out,
    w_in,
    w_back,
    b_query,
    b_value,
    b_out,
    b_in,
    b_back,
    gain_attn,
    shift_attn,
    gain_ffn,
    shift_ffn,
    out_rows,
    out_grad,
    out_pieces,
    out_vectors,
    wqkv,
    wo,
    wi,
    wb,
    bias_q,
    bias_v,
    bias_i,
    x_s,
    dy_s,
    normed,
    qkv,
    mixed,
    lse,
    hidden,
    normed2,
    flip2,
    ffn,
    dn2,
    act,
    dpre,
    flip,
    wide_a,
    wide_b,
    dattn,
    dmixed,
    result,
    probs_t,
    dscores_t,
    held,
    other,
    pair,
    landed,
    vec,
    vec_other,
    vec_landed,
    load_sem,
    weight_send,
    weight_recv,
    pair_send,
    pair_recv,
    send_sem,
    recv_sem,
    store_sem,
    vec_send,
    vec_recv,
    row_send,
    row_recv,
    row_sem,
):
    me = lax.axis_index("dp")
    core = lax.axis_index("tensor")
    width, local = size.width, size.local
    bits, halving, sends, pieces = size.bits, size.halving, size.sends, size.pieces
    orders = bit_orders(bits, halving)
    my_rows = pl.ds(pl.multiple_of(core * SEQ, SEQ), SEQ)

    def colour_of(piece):
        place = lax.rem(piece, 13)
        third = (place == 4) | (place == 8) | (place == 12)
        return jnp.where(third, 2, lax.rem(place, 2))

    def bit_at(colour, level):
        strides = [1 << order[level] for order in orders]
        stride = jnp.where(
            colour == 0, strides[0], jnp.where(colour == 1, strides[1], strides[2])
        )
        return stride, lax.rem(lax.div(me, stride), 2)

    def base_of(colour, level):
        base = 0
        for earlier in range(min(level, halving)):
            base = base + bit_at(colour, earlier)[1] * (SHARDS >> (earlier + 1))
        return base

    def landing_of(level):
        if level < halving:
            return SHARDS - (SHARDS >> level), SHARDS >> (level + 1)
        return SHARDS - (SHARDS >> halving) + level - halving, SHARDS >> halving

    def level_of(step):
        return step if step < bits else sends - 1 - step

    def copy(piece, step):
        colour = colour_of(piece)
        level = level_of(step)
        stride, bit = bit_at(colour, level)
        base = base_of(colour, level)
        if level < halving:
            half = SHARDS >> (level + 1)
            start = base + ((1 - bit) if step < bits else bit) * half
        else:
            half = SHARDS >> halving
            start = base
        if step < bits:
            source = held.at[piece, pl.ds(start, half)]
            target = landed.at[piece, pl.ds(landing_of(level)[0], half)]
        else:
            source = pair.at[piece, pl.ds(start, half)]
            target = source
        return pltpu.make_async_remote_copy(
            src_ref=source,
            dst_ref=target,
            send_sem=send_sem.at[piece, step],
            recv_sem=recv_sem.at[piece, step],
            device_id={"dp": me + (1 - 2 * bit) * stride},
            device_id_type=MESH,
        )

    def add_level(piece, level):
        colour = colour_of(piece)
        base = base_of(colour, level + 1)
        place, half = landing_of(level)
        total = held if level < bits - 1 else pair
        group = min(half, 4)

        def some(index, carry):
            mine = held[piece, pl.ds(base + index * group, group)]
            theirs = landed[piece, pl.ds(place + index * group, group)]
            total[piece, pl.ds(base + index * group, group)] = mine + theirs
            return carry

        lax.fori_loop(0, half // group, some, 0)

    def pair_copy(piece):
        return pltpu.make_async_remote_copy(
            src_ref=other.at[piece],
            dst_ref=pair.at[piece],
            send_sem=pair_send.at[piece],
            recv_sem=pair_recv.at[piece],
            device_id={"tensor": 1 - core},
            device_id_type=MESH,
        )

    def store(piece):
        return pltpu.make_async_copy(pair.at[piece], out_pieces.at[piece], store_sem.at[piece])

    def advance(piece, step):
        if step == 0:
            pair_copy(piece).wait_recv()

            def some(index, carry):
                shards = pl.ds(index * 4, 4)
                held[piece, shards] = held[piece, shards] + pair[piece, shards]
                return carry

            lax.fori_loop(0, SHARDS // 4, some, 0)
        else:
            copy(piece, step - 1).wait_recv()
            if halving < step <= bits:
                copy(piece, step - 1).wait_send()
            if step <= bits:
                add_level(piece, step - 1)
        if step < sends:
            copy(piece, step).start()
        else:
            store(piece).start()
            for earlier in early_sends:
                copy(piece, earlier).wait_send()
            pair_copy(piece).wait_send()

    early_sends = [step for step in range(sends - 1) if not halving <= step < bits]

    def offset_of(step):
        return LAG * step + (DELAY if step >= bits else 0)

    def tick(time, carry):
        for step in range(sends + 1):
            piece = time - offset_of(step)

            @pl.when((piece >= 0) & (piece < pieces))
            def _():
                advance(piece, step)

        return carry

    def ticks(first, amount):
        lax.fori_loop(first, first + amount, tick, 0)

    def send_pairs(first, amount):
        def one(piece, carry):
            pair_copy(piece).start()
            return carry

        lax.fori_loop(first, first + amount, one, 0)

    def load(source, target, place):
        return pltpu.make_async_copy(source, target, load_sem.at[place])

    loads = [
        load(tokens.at[my_rows], x_s, 0),
        load(cotangent.at[my_rows], dy_s, 1),
        load(w_query, wqkv.at[0, :, pl.ds(0, local)], 2),
        load(w_key, wqkv.at[0, :, pl.ds(local, local)], 3),
        load(w_value, wqkv.at[0, :, pl.ds(2 * local, local)], 4),
        load(w_out, wo.at[pl.ds(0, local)], 5),
        load(w_in, wi.at[0], 6),
        load(w_back, wb.at[0], 7),
    ]
    for item in loads:
        item.start()

    barrier = pltpu.get_barrier_semaphore()
    pl.semaphore_signal(barrier, inc=1, device_id={"tensor": 1 - core}, device_id_type=MESH)
    for bit in range(bits):
        mine = lax.rem(lax.div(me, 1 << bit), 2)
        pl.semaphore_signal(
            barrier,
            inc=1,
            device_id={"dp": me + (1 - 2 * mine) * (1 << bit)},
            device_id_type=MESH,
        )
    pl.semaphore_wait(barrier, bits + 1)

    def to_partner(source, target, place):
        return pltpu.make_async_remote_copy(
            src_ref=source,
            dst_ref=target,
            send_sem=weight_send.at[place],
            recv_sem=weight_recv.at[place],
            device_id={"tensor": 1 - core},
            device_id_type=MESH,
        )

    gathers = [
        to_partner(b_query, bias_q, 0),
        to_partner(b_value, bias_v, 1),
        to_partner(b_in, bias_i, 2),
        to_partner(w_query, wqkv.at[1, :, pl.ds(0, local)], 3),
        to_partner(w_key, wqkv.at[1, :, pl.ds(local, local)], 4),
        to_partner(w_value, wqkv.at[1, :, pl.ds(2 * local, local)], 5),
        to_partner(w_out, wo.at[pl.ds(local, local)], 6),
        to_partner(w_in, wi.at[1], 7),
        to_partner(w_back, wb.at[1], 8),
    ]
    for item in gathers:
        item.start()

    vec[...] = jnp.zeros_like(vec)
    vec_other[...] = jnp.zeros_like(vec_other)
    ffn[...] = jnp.zeros_like(ffn)
    dn2[...] = jnp.zeros_like(dn2)

    small = 128
    loads[0].wait()

    def first_norm(tile, carry):
        rows = pl.ds(pl.multiple_of(tile * small, small), small)
        unit, rstd = norm_parts(x_s[rows].astype(F32))
        normed[rows] = (unit * row_of(gain_attn) + row_of(shift_attn)).astype(BF16)
        return carry

    lax.fori_loop(0, SEQ // small, first_norm, 0)

    for half in range(2):
        if half == 0:
            for item in loads[2:5]:
                item.wait()
            bias_query, bias_value = b_query, b_value
        else:
            for item in gathers[0:2] + gathers[3:6]:
                item.wait_recv()
            bias_query, bias_value = bias_q, bias_v
        qkv[half, :, 0:local] = (
            matmul(normed[...], wqkv[half, :, 0:local]) + row_of(bias_query)
        ).astype(BF16)
        qkv[half, :, local : 2 * local] = matmul(
            normed[...], wqkv[half, :, local : 2 * local]
        ).astype(BF16)
        qkv[half, :, 2 * local : 3 * local] = (
            matmul(normed[...], wqkv[half, :, 2 * local : 3 * local]) + row_of(bias_value)
        ).astype(BF16)

    pairs_half = local // LANES
    scale = HEAD ** (-0.5)
    lane = lax.broadcasted_iota(jnp.int32, (1, LANES), 1)
    masks = [
        jnp.where((lane >= part * HEAD) & (lane < (part + 1) * HEAD), 1.0, 0.0).astype(BF16)
        for part in range(LANES // HEAD)
    ]
    queries = 128

    def columns(index, group):
        return pl.ds(pl.multiple_of(group * local + index * LANES, LANES), LANES)

    def attend(index, carry):
        half, place = lax.div(index, pairs_half), lax.rem(index, pairs_half)
        key = qkv[half, :, columns(place, 1)]
        value = qkv[half, :, columns(place, 2)]
        total = None
        for part, mask in enumerate(masks):
            for tile in range(SEQ // queries):
                rows = slice(tile * queries, (tile + 1) * queries)
                query = qkv[half, rows, columns(place, 0)] * (mask * scale).astype(BF16)
                scores = matmul_right(key, query)
                top = jnp.max(scores, axis=0, keepdims=True)
                expo = jnp.exp(scores - top)
                amount = jnp.sum(expo, axis=0, keepdims=True)
                lse[index * 2 + part, :, rows] = top + jnp.log(amount)
                probs_t[part, :, rows] = (expo * (1.0 / amount)).astype(BF16)
            term = matmul_left(probs_t[part], value * mask)
            total = term if total is None else total + term
        mixed[:, pl.ds(pl.multiple_of(index * LANES, LANES), LANES)] = total.astype(BF16)
        return carry

    lax.fori_loop(0, 2 * pairs_half, attend, 0)

    loads[5].wait()
    gathers[6].wait_recv()
    hidden[...] = matmul(mixed[...], wo[...])

    def second_norm(tile, carry):
        rows = pl.ds(pl.multiple_of(tile * small, small), small)
        whole = x_s[rows].astype(F32) + (hidden[rows] + row_of(b_out))
        hidden[rows] = whole
        unit, rstd = norm_parts(whole)
        normed2[rows] = (unit * row_of(gain_ffn) + row_of(shift_ffn)).astype(BF16)
        return carry

    lax.fori_loop(0, SEQ // small, second_norm, 0)
    flip2[...] = normed2[...].T

    loads[1].wait()
    loads[6].wait()
    loads[7].wait()
    gathers[2].wait_recv()
    gathers[7].wait_recv()
    gathers[8].wait_recv()
    ones = jnp.ones((16, SEQ), BF16)
    fine = 32
    tall = 256

    def hand_in(target, first, grad, kind, part):
        wide = 2 * LANES
        if kind == "in":
            for side in range(2):
                target[first + 2 * part + side] = (
                    grad[:, side * LANES : (side + 1) * LANES]
                    .astype(BF16)
                    .reshape(SHARDS, ROWS, LANES)
                )
        else:
            blocks = grad.shape[0] // (ROWS * SHARDS // 2)
            for block in range(blocks):
                rows = slice(block * ROWS * SHARDS // 2, (block + 1) * ROWS * SHARDS // 2)
                for side in range(2):
                    target[
                        first + (width // wide) * block + part,
                        side * (SHARDS // 2) : (side + 1) * (SHARDS // 2),
                    ] = (
                        grad[rows, side * LANES : (side + 1) * LANES]
                        .astype(BF16)
                        .reshape(SHARDS // 2, ROWS, LANES)
                    )

    def feed(chunk, half, slots):
        begin = pl.multiple_of(chunk * width, width)
        units = pl.ds(begin, width)
        bias_row = b_in if half == 0 else bias_i
        target = held if half == 0 else other
        first = chunk * size.per_chunk

        def rows_tile(tile, carry):
            rows = pl.ds(pl.multiple_of(tile * tall, tall), tall)
            wide_a[...] = matmul(normed2[rows], wi[half, :, units])
            wide_b[...] = matmul_right(dy_s[rows], wb[half, units, :])

            def inner(step, carry):
                piece = pl.ds(pl.multiple_of(step * fine, fine), fine)
                there = pl.ds(pl.multiple_of(tile * tall + step * fine, fine), fine)
                pre = wide_a[piece] + bias_row[units].reshape(1, -1)
                phi = 0.5 * (1.0 + lax.erf(pre * 0.7071067811865476))
                act[there] = (pre * phi).astype(BF16)
                slope = phi + pre * jnp.exp(-0.5 * pre * pre) * 0.3989422804014327
                dpre[there] = (wide_b[piece] * slope).astype(BF16)
                return carry

            lax.fori_loop(0, tall // fine, inner, 0)
            return carry

        lax.fori_loop(0, SEQ // tall, rows_tile, 0)
        flip[...] = act[...].T
        slots(0)
        for part in range(width // 256):
            cols = slice(part * 256, (part + 1) * 256)
            hand_in(target, first, matmul(flip2[...], dpre[:, cols]), "in", part)
        for part in range(width // 256):
            cols = slice(part * 256, (part + 1) * 256)
            hand_in(target, first + size.block, matmul(flip[...], dy_s[:, cols]), "out", part)
        slots(1)
        if half == 0:
            slots(2)
        ffn[...] += matmul(act[...], wb[half, units, :])
        dn2[...] += matmul_right(dpre[...], wi[half, :, units])
        sums = matmul(ones, dpre[...])[0:1]
        (vec if half == 0 else vec_other)[pl.ds(7 + chunk, 1)] = sums

    def feed_both(chunk, carry):
        def slots(offset, half):
            def place(index):
                first = HEAD_START + (chunk - 1) * 4 * EACH + (offset + index) * EACH
                if index == 1 and half == 1:
                    send_pairs(chunk * size.per_chunk, size.per_chunk)
                if index == 2:
                    lax.fori_loop(0, jnp.where(chunk > 0, 0, HEAD_START), tick, 0)
                else:
                    lax.fori_loop(first, jnp.where(chunk > 0, first + EACH, first), tick, 0)

            return place

        feed(chunk, 1, slots(0, 1))
        feed(chunk, 0, slots(2, 0))
        return carry

    lax.fori_loop(0, size.chunks, feed_both, 0)
    time = HEAD_START + (size.chunks - 1) * 4 * EACH

    tiny = 64

    def second_back(tile, carry):
        sum_gain, sum_shift, sum_out = carry
        rows = pl.ds(pl.multiple_of(tile * tiny, tiny), tiny)
        whole = hidden[rows]
        result[rows] = (whole + (ffn[rows] + row_of(b_back))).astype(BF16)
        unit, rstd = norm_parts(whole)
        grad = dn2[rows]
        dhidden = dy_s[rows].astype(F32) + norm_back(grad * row_of(gain_ffn), unit, rstd)
        dn2[rows] = dhidden
        rounded = dhidden.astype(BF16)
        dattn[rows] = rounded
        return (
            sum_gain + fold(grad * unit),
            sum_shift + fold(grad),
            sum_out + fold(rounded.astype(F32)),
        )

    zero = jnp.zeros((8, width), F32)
    sum_gain, sum_shift, sum_out = lax.fori_loop(
        0, SEQ // tiny, second_back, (zero, zero, zero)
    )

    def both(row, value):
        vec[row : row + 1] = value
        vec_other[row : row + 1] = value

    both(0, jnp.sum(sum_out, axis=0, keepdims=True))
    both(1, matmul(ones, dy_s[...])[0:1])
    both(4, jnp.sum(sum_gain, axis=0, keepdims=True))
    both(5, jnp.sum(sum_shift, axis=0, keepdims=True))

    def row_copies(source, target, place):
        return (
            pltpu.make_async_copy(source, target.at[my_rows], row_sem.at[place]),
            pltpu.make_async_remote_copy(
                src_ref=source,
                dst_ref=target.at[my_rows],
                send_sem=row_send.at[place],
                recv_sem=row_recv.at[place],
                device_id={"tensor": 1 - core},
                device_id_type=MESH,
            ),
        )

    result_copies = row_copies(result, out_rows, 0)
    for item in result_copies:
        item.start()
    ticks(time, NORM_TICKS)
    time += NORM_TICKS

    flip[...] = mixed[...].T
    for part in range(width // 256):
        cols = slice(part * 256, (part + 1) * 256)
        grad = matmul(flip[...], dattn[:, cols])
        hand_in(held, size.first_out, grad[0:local], "out", part)
        hand_in(other, size.first_out, grad[local:], "out", part)
    send_pairs(size.first_out, size.first_qkv - size.first_out)
    dmixed[...] = matmul_right(dattn[...], wo[...]).astype(BF16)
    ticks(time, OUT_TICKS)
    time += OUT_TICKS

    def attend_back(index, carry):
        half, place = lax.div(index, pairs_half), lax.rem(index, pairs_half)
        here = pl.ds(pl.multiple_of(index * LANES, LANES), LANES)
        key = qkv[half, :, columns(place, 1)]
        value = qkv[half, :, columns(place, 2)]
        dquery, dkey, dvalue = None, None, None
        for part, mask in enumerate(masks):
            for tile in range(SEQ // queries):
                rows = slice(tile * queries, (tile + 1) * queries)
                query = qkv[half, rows, columns(place, 0)] * (mask * scale).astype(BF16)
                scores = matmul_right(key, query)
                probs = jnp.exp(scores - lse[index * 2 + part, :, rows])
                dprobs = matmul_right(value, dmixed[rows, here] * mask)
                inner = jnp.sum(dprobs * probs, axis=0, keepdims=True)
                probs_t[part, :, rows] = probs.astype(BF16)
                dscores_t[part, :, rows] = (probs * (dprobs - inner)).astype(BF16)
            query = qkv[half, :, columns(place, 0)] * (mask * scale).astype(BF16)
            terms = (
                matmul_left(dscores_t[part], key * mask),
                matmul(dscores_t[part], query),
                matmul(probs_t[part], dmixed[:, here] * mask),
            )
            if dquery is None:
                dquery, dkey, dvalue = terms
            else:
                dquery, dkey, dvalue = dquery + terms[0], dkey + terms[1], dvalue + terms[2]
        qkv[half, :, columns(place, 0)] = (dquery * scale).astype(BF16)
        qkv[half, :, columns(place, 1)] = dkey.astype(BF16)
        qkv[half, :, columns(place, 2)] = dvalue.astype(BF16)
        ticks(time + index * PAIR_TICKS, PAIR_TICKS)
        return carry

    lax.fori_loop(0, 2 * pairs_half, attend_back, 0)
    time += 2 * pairs_half * PAIR_TICKS

    flip[...] = normed[...].T
    for half in (1, 0):
        target = held if half == 0 else other
        for part in range(3 * local // LANES):
            cols = slice(part * LANES, (part + 1) * LANES)
            grad = matmul(flip[...], qkv[half, :, cols])
            target[size.first_qkv + part] = grad.astype(BF16).reshape(SHARDS, ROWS, LANES)
        if half == 1:
            send_pairs(size.first_qkv, size.pieces - size.first_qkv)
        amount = min(QKV_TICKS, size.first_qkv - time) if half == 1 else QKV_TICKS + 1
        ticks(time, amount)
        time += amount
    for half in range(2):
        table = vec if half == 0 else vec_other
        table[6:7, 0:local] = matmul(ones, qkv[half, :, 0:local])[0:1]
        table[6:7, local : 2 * local] = matmul(ones, qkv[half, :, 2 * local : 3 * local])[0:1]
    hidden[...] = matmul_right(qkv[0], wqkv[0])
    hidden[...] += matmul_right(qkv[1], wqkv[1])
    ticks(time, QKV_TICKS)
    time += QKV_TICKS

    def first_back(tile, carry):
        sum_gain, sum_shift = carry
        rows = pl.ds(pl.multiple_of(tile * tiny, tiny), tiny)
        unit, rstd = norm_parts(x_s[rows].astype(F32))
        grad = hidden[rows]
        ffn[rows] = dn2[rows] + norm_back(grad * row_of(gain_attn), unit, rstd)
        return sum_gain + fold(grad * unit), sum_shift + fold(grad)

    sum_gain, sum_shift = lax.fori_loop(0, SEQ // tiny, first_back, (zero, zero))
    both(2, jnp.sum(sum_gain, axis=0, keepdims=True))
    both(3, jnp.sum(sum_shift, axis=0, keepdims=True))
    grad_copies = row_copies(ffn, out_grad, 1)
    for item in grad_copies:
        item.start()

    def vector_copy(step):
        if step == 0:
            source, partner = vec_other, {"tensor": 1 - core}
        else:
            bit = lax.rem(lax.div(me, 1 << (step - 1)), 2)
            source, partner = vec, {"dp": me + (1 - 2 * bit) * (1 << (step - 1))}
        return pltpu.make_async_remote_copy(
            src_ref=source,
            dst_ref=vec_landed.at[step],
            send_sem=vec_send.at[step],
            recv_sem=vec_recv.at[step],
            device_id=partner,
            device_id_type=MESH,
        )

    for step in range(bits + 1):
        vector_copy(step).start()
        ticks(time, 3)
        time += 3
        vector_copy(step).wait()
        vec[...] += vec_landed[step]
    vector_store = pltpu.make_async_copy(vec, out_vectors, row_sem.at[2])
    vector_store.start()
    ticks(time, pieces + offset_of(sends) - time)

    def finish(piece, carry):
        copy(piece, sends - 1).wait_send()
        store(piece).wait()
        return carry

    lax.fori_loop(0, pieces, finish, 0)
    for item in gathers:
        item.wait_send()
    for local_copy, remote_copy in (result_copies, grad_copies):
        local_copy.wait()
        remote_copy.wait()
    vector_store.wait()


def run_layer(size, arrays, vectors):
    width, local, hidden = size.width, size.local, size.hidden
    rows = arrays[0].shape[0]
    steps = size.sends
    rank = pltpu.SemaphoreType
    any_space = pl.BlockSpec(memory_space=pl.ANY)
    in_vmem = pl.BlockSpec(memory_space=pltpu.VMEM)
    piece_shape = (size.pieces, SHARDS, ROWS, LANES)
    scratch = [
        pltpu.VMEM((2, width, 3 * local), BF16),
        pltpu.VMEM((2 * local, width), BF16),
        pltpu.VMEM((2, width, hidden), BF16),
        pltpu.VMEM((2, hidden, width), BF16),
        pltpu.VMEM((local,), F32),
        pltpu.VMEM((local,), F32),
        pltpu.VMEM((hidden,), F32),
        pltpu.VMEM((SEQ, width), BF16),
        pltpu.VMEM((SEQ, width), BF16),
        pltpu.VMEM((SEQ, width), BF16),
        pltpu.VMEM((2, SEQ, 3 * local), BF16),
        pltpu.VMEM((SEQ, width), BF16),
        pltpu.VMEM((2 * local // HEAD, 1, SEQ), F32),
        pltpu.VMEM((SEQ, width), F32),
        pltpu.VMEM((SEQ, width), BF16),
        pltpu.VMEM((width, SEQ), BF16),
        pltpu.VMEM((SEQ, width), F32),
        pltpu.VMEM((SEQ, width), F32),
        pltpu.VMEM((SEQ, width), BF16),
        pltpu.VMEM((SEQ, width), BF16),
        pltpu.VMEM((width, SEQ), BF16),
        pltpu.VMEM((256, width), F32),
        pltpu.VMEM((256, width), F32),
        pltpu.VMEM((SEQ, width), BF16),
        pltpu.VMEM((SEQ, width), BF16),
        pltpu.VMEM((SEQ, width), BF16),
        pltpu.VMEM((LANES // HEAD, SEQ, SEQ), BF16),
        pltpu.VMEM((LANES // HEAD, SEQ, SEQ), BF16),
        pltpu.VMEM(piece_shape, BF16),
        pltpu.VMEM(piece_shape, BF16),
        pltpu.VMEM(piece_shape, BF16),
        pltpu.VMEM((size.pieces, size.landing, ROWS, LANES), BF16),
        pltpu.VMEM((16, width), F32),
        pltpu.VMEM((16, width), F32),
        pltpu.VMEM((size.bits + 1, 16, width), F32),
        rank.DMA((8,)),
        rank.DMA((9,)),
        rank.DMA((9,)),
        rank.DMA((size.pieces,)),
        rank.DMA((size.pieces,)),
        rank.DMA((size.pieces, steps)),
        rank.DMA((size.pieces, steps)),
        rank.DMA((size.pieces,)),
        rank.DMA((size.bits + 1,)),
        rank.DMA((size.bits + 1,)),
        rank.DMA((2,)),
        rank.DMA((2,)),
        rank.DMA((3,)),
    ]
    return pl.pallas_call(
        functools.partial(layer_kernel, size),
        out_shape=(
            jax.ShapeDtypeStruct((rows, width), BF16),
            jax.ShapeDtypeStruct((rows, width), F32),
            jax.ShapeDtypeStruct(piece_shape, BF16),
            jax.ShapeDtypeStruct((16, width), F32),
        ),
        in_specs=[any_space] * len(arrays) + [in_vmem] * len(vectors),
        out_specs=(any_space,) * 4,
        scratch_shapes=scratch,
        compiler_params=pltpu.CompilerParams(
            collective_id=0, has_side_effects=True, vmem_limit_bytes=67043328
        ),
        name="layer",
    )(*arrays, *vectors)


def unpack_kernel(size, pieces, vectors_in, rows_in, grad_in, *refs):
    g_wq, g_wk, g_wv, g_wo, g_wi, g_wb, rows_end, grad_end = refs[:8]
    rows_out = refs[8:17]
    held, s_in, s_back, s_qkv, s_out, vectors, rows, grad, sem, out_sem, side_sem = refs[17:]
    width, local = size.width, size.local
    wide = 2 * LANES
    half_rows = ROWS * SHARDS // 2
    spans = []
    for chunk in range(size.chunks):
        first = chunk * size.per_chunk
        spans.append((first, size.block))
        spans.append((first + size.block, size.block))
    spans.append((size.first_out, size.first_qkv - size.first_out))
    for index in range(3):
        spans.append((size.first_qkv + index * local // LANES, local // LANES))
    copies = []
    for index, (first, amount) in enumerate(spans):
        item = pltpu.make_async_copy(
            pieces.at[pl.ds(first, amount)], held.at[pl.ds(first, amount)], sem.at[index]
        )
        item.start()
        copies.append(item)
    sides = [
        pltpu.make_async_copy(source, target, side_sem.at[index])
        for index, (source, target) in enumerate(
            ((vectors_in, vectors), (rows_in, rows), (grad_in, grad))
        )
    ]
    for item in sides:
        item.start()
    sides[0].wait()
    for ref, row, begin, amount in zip(
        rows_out,
        (6, 6, 0, 7, 1, 2, 3, 4, 5),
        (0, local, 0, 0, 0, 0, 0, 0, 0),
        (local, local, width, width, width, width, width, width, width),
    ):
        for chunk in range(ref.shape[0] // amount):
            ref[chunk * amount : (chunk + 1) * amount] = vectors[
                row + chunk, begin : begin + amount
            ]

    outs = []

    def put(source, target):
        item = pltpu.make_async_copy(source, target, out_sem.at[len(outs)])
        item.start()
        outs.append(item)

    def columns(first, amount, target, begin):
        for index in range(amount):
            target[:, begin + index * LANES : begin + (index + 1) * LANES] = (
                held[first + index].reshape(SHARDS * ROWS, LANES).astype(F32)
            )

    def blocks(first, rows, target, begin):
        for block in range(rows // half_rows):
            for part in range(width // wide):
                for side in range(2):
                    value = held[
                        first + block * (width // wide) + part,
                        side * (SHARDS // 2) : (side + 1) * (SHARDS // 2),
                    ]
                    target[
                        begin + block * half_rows : begin + (block + 1) * half_rows,
                        part * wide + side * LANES : part * wide + (side + 1) * LANES,
                    ] = value.reshape(half_rows, LANES).astype(F32)

    at = 0
    for chunk in range(size.chunks):
        first = chunk * size.per_chunk
        copies[at].wait()
        columns(first, size.block, s_in.at[chunk], 0)
        put(s_in.at[chunk], g_wi.at[:, pl.ds(chunk * width, width)])
        copies[at + 1].wait()
        blocks(first + size.block, width, s_back, chunk * width)
        put(
            s_back.at[pl.ds(chunk * width, width)],
            g_wb.at[pl.ds(chunk * width, width)],
        )
        at += 2
    copies[at].wait()
    blocks(size.first_out, local, s_out, 0)
    put(s_out, g_wo)
    at += 1
    for index, target in enumerate((g_wq, g_wk, g_wv)):
        copies[at].wait()
        columns(size.first_qkv + index * local // LANES, local // LANES, s_qkv.at[index], 0)
        put(s_qkv.at[index], target)
        at += 1
    sides[1].wait()
    put(rows, rows_end)
    sides[2].wait()
    put(grad, grad_end)
    for item in outs:
        item.wait()


def unpack(size, pieces, vectors, block_rows, grad_rows):
    width, local, hidden = size.width, size.local, size.hidden
    any_space = pl.BlockSpec(memory_space=pl.ANY)
    in_vmem = pl.BlockSpec(memory_space=pltpu.VMEM)
    matrices = [(width, local)] * 3 + [(local, width), (width, hidden), (hidden, width)]
    rows = [local, local, width, hidden, width, width, width, width, width]
    transfers = 2 * size.chunks + 6
    return pl.pallas_call(
        functools.partial(unpack_kernel, size),
        out_shape=tuple(jax.ShapeDtypeStruct(shape, F32) for shape in matrices)
        + tuple(jax.ShapeDtypeStruct(item.shape, item.dtype) for item in (block_rows, grad_rows))
        + tuple(jax.ShapeDtypeStruct((amount,), F32) for amount in rows),
        in_specs=[any_space] * 4,
        out_specs=(any_space,) * 8 + (in_vmem,) * 9,
        scratch_shapes=[
            pltpu.VMEM(pieces.shape, BF16),
            pltpu.VMEM((size.chunks, width, width), F32),
            pltpu.VMEM((hidden, width), F32),
            pltpu.VMEM((3, width, local), F32),
            pltpu.VMEM((local, width), F32),
            pltpu.VMEM(vectors.shape, F32),
            pltpu.VMEM(block_rows.shape, BF16),
            pltpu.VMEM(grad_rows.shape, F32),
            pltpu.SemaphoreType.DMA((transfers,)),
            pltpu.SemaphoreType.DMA((transfers,)),
            pltpu.SemaphoreType.DMA((3,)),
        ],
        compiler_params=pltpu.CompilerParams(vmem_limit_bytes=67043328),
        name="unpack",
    )(pieces, vectors, block_rows, grad_rows)


def on_device(
    tokens,
    cotangent,
    w_query,
    b_query,
    w_key,
    w_value,
    b_value,
    w_out,
    b_out,
    w_in,
    b_in,
    w_back,
    b_back,
    gain_attn,
    shift_attn,
    gain_ffn,
    shift_ffn,
):
    size = Sizes(lax.axis_size("dp"), tokens, w_query, w_in)
    assert tokens.shape[0] == SEQ * lax.axis_size("tensor") and lax.axis_size("tensor") == 2
    assert size.count == 1 << size.bits and size.width == SHARDS * ROWS
    vectors = (
        b_query,
        b_value,
        b_out,
        b_in,
        b_back,
        gain_attn,
        shift_attn,
        gain_ffn,
        shift_ffn,
    )
    rows, grad_rows, pieces, sums = run_layer(
        size,
        (tokens, cotangent, w_query, w_key, w_value, w_out, w_in, w_back),
        vectors,
    )
    outs = unpack(size, pieces, sums, rows, grad_rows)
    g_wq, g_wk, g_wv, g_wo, g_wi, g_wb = outs[:6]
    g_bq, g_bv, g_bo, g_bi, g_bb, g_ga, g_sa, g_gf, g_sf = outs[8:]
    return (
        *outs[6:8],
        g_wq,
        g_bq,
        g_wk,
        g_wv,
        g_bv,
        g_wo,
        g_bo,
        g_wi,
        g_bi,
        g_wb,
        g_bb,
        g_ga,
        g_sa,
        g_gf,
        g_sf,
    )


def solution(mesh):
    columns, rows, vector, whole = P(None, "tensor"), P("tensor", None), P("tensor"), P()
    weights = (
        columns,
        vector,
        columns,
        columns,
        vector,
        rows,
        whole,
        columns,
        vector,
        rows,
        whole,
        whole,
        whole,
        whole,
        whole,
    )
    data = (P("dp", None), P("dp", None))
    return jax.shard_map(
        on_device, mesh=mesh, in_specs=data + weights, out_specs=data + weights, check_vma=False
    )
```

```python
import functools

import jax
import jax.numpy as jnp
from jax import lax
from jax.experimental import pallas as pl
from jax.experimental.pallas import tpu as pltpu
from jax.sharding import PartitionSpec as P

HEAD = 64
SEQ = 512
EPS = 1e-12
SHARDS = 16
ROWS = 48
LANES = 128
LAG = 4
HEAD_START = 2
EACH = 2
NORM_TICKS = 2
OUT_TICKS = 2
PAIR_TICKS = 2
QKV_TICKS = 2
DELAY = 0
MESH = pl.DeviceIdType.MESH
F32 = jnp.float32
BF16 = jnp.bfloat16


def matmul(left, right):
    return jnp.dot(left, right, preferred_element_type=F32)


def matmul_left(left, right):
    return lax.dot_general(left, right, (((0,), (0,)), ((), ())), preferred_element_type=F32)


def matmul_right(left, right):
    return lax.dot_general(left, right, (((1,), (1,)), ((), ())), preferred_element_type=F32)


def norm_parts(value):
    mean = jnp.mean(value, axis=-1, keepdims=True)
    centred = value - mean
    rstd = lax.rsqrt(jnp.mean(centred * centred, axis=-1, keepdims=True) + EPS)
    return centred * rstd, rstd


def norm_back(scaled, unit, rstd):
    return rstd * (
        scaled
        - jnp.mean(scaled, axis=-1, keepdims=True)
        - unit * jnp.mean(scaled * unit, axis=-1, keepdims=True)
    )


def row_of(ref):
    return ref[...].reshape(1, -1)


def fold(value):
    return jnp.sum(value.reshape(value.shape[0] // 8, 8, value.shape[1]), axis=0)


class Sizes:
    def __init__(self, count, tokens, w_query, w_in):
        self.count = count
        self.bits = count.bit_length() - 1
        self.halving = min(self.bits, SHARDS.bit_length() - 1)
        self.sends = self.bits + self.halving
        self.width = tokens.shape[1]
        self.local = w_query.shape[1]
        self.hidden = w_in.shape[1]
        self.chunks = self.hidden // self.width
        self.block = self.width // LANES
        self.per_chunk = 2 * self.block
        self.first_out = self.chunks * self.per_chunk
        self.first_qkv = self.first_out + self.local // LANES
        self.pieces = self.first_qkv + 3 * self.local // LANES
        self.landing = SHARDS - (SHARDS >> self.halving) + self.bits - self.halving


def bit_orders(bits, halving):
    low = list(range(halving))
    high = list(range(halving, bits))
    if halving < 3:
        return [low + high] * 3
    return [low + high, [1, 0] + low[2:] + high, low[2:] + low[:2] + high]


def layer_kernel(
    size,
    tokens,
    cotangent,
    w_query,
    w_key,
    w_value,
    w_out,
    w_in,
    w_back,
    b_query,
    b_value,
    b_out,
    b_in,
    b_back,
    gain_attn,
    shift_attn,
    gain_ffn,
    shift_ffn,
    out_rows,
    out_grad,
    out_pieces,
    out_vectors,
    wqkv,
    wo,
    wi,
    wb,
    bias_q,
    bias_v,
    bias_i,
    x_s,
    dy_s,
    normed,
    qkv,
    mixed,
    lse,
    hidden,
    normed2,
    flip2,
    ffn,
    dn2,
    act,
    dpre,
    flip,
    wide_a,
    wide_b,
    dattn,
    dmixed,
    probs_t,
    dscores_t,
    held,
    other,
    pair,
    landed,
    vec,
    vec_other,
    vec_landed,
    load_sem,
    weight_send,
    weight_recv,
    pair_send,
    pair_recv,
    send_sem,
    recv_sem,
    store_sem,
    vec_send,
    vec_recv,
    row_send,
    row_recv,
    row_sem,
):
    me = lax.axis_index("dp")
    core = lax.axis_index("tensor")
    width, local = size.width, size.local
    bits, halving, sends, pieces = size.bits, size.halving, size.sends, size.pieces
    orders = bit_orders(bits, halving)
    my_rows = pl.ds(pl.multiple_of(core * SEQ, SEQ), SEQ)

    def colour_of(piece):
        place = lax.rem(piece, 13)
        third = (place == 4) | (place == 8) | (place == 12)
        return jnp.where(third, 2, lax.rem(place, 2))

    def bit_at(colour, level):
        strides = [1 << order[level] for order in orders]
        stride = jnp.where(
            colour == 0, strides[0], jnp.where(colour == 1, strides[1], strides[2])
        )
        return stride, lax.rem(lax.div(me, stride), 2)

    def base_of(colour, level):
        base = 0
        for earlier in range(min(level, halving)):
            base = base + bit_at(colour, earlier)[1] * (SHARDS >> (earlier + 1))
        return base

    def landing_of(level):
        if level < halving:
            return SHARDS - (SHARDS >> level), SHARDS >> (level + 1)
        return SHARDS - (SHARDS >> halving) + level - halving, SHARDS >> halving

    def level_of(step):
        return step if step < bits else sends - 1 - step

    def copy(piece, step):
        colour = colour_of(piece)
        level = level_of(step)
        stride, bit = bit_at(colour, level)
        base = base_of(colour, level)
        if level < halving:
            half = SHARDS >> (level + 1)
            start = base + ((1 - bit) if step < bits else bit) * half
        else:
            half = SHARDS >> halving
            start = base
        if step < bits:
            source = held.at[piece, pl.ds(start, half)]
            target = landed.at[piece, pl.ds(landing_of(level)[0], half)]
        else:
            source = pair.at[piece, pl.ds(start, half)]
            target = source
        return pltpu.make_async_remote_copy(
            src_ref=source,
            dst_ref=target,
            send_sem=send_sem.at[piece, step],
            recv_sem=recv_sem.at[piece, step],
            device_id={"dp": me + (1 - 2 * bit) * stride},
            device_id_type=MESH,
        )

    def add_level(piece, level):
        colour = colour_of(piece)
        base = base_of(colour, level + 1)
        place, half = landing_of(level)
        total = held if level < bits - 1 else pair
        group = min(half, 4)

        def some(index, carry):
            mine = held[piece, pl.ds(base + index * group, group)]
            theirs = landed[piece, pl.ds(place + index * group, group)]
            total[piece, pl.ds(base + index * group, group)] = mine + theirs
            return carry

        lax.fori_loop(0, half // group, some, 0)

    def pair_copy(piece):
        return pltpu.make_async_remote_copy(
            src_ref=other.at[piece],
            dst_ref=pair.at[piece],
            send_sem=pair_send.at[piece],
            recv_sem=pair_recv.at[piece],
            device_id={"tensor": 1 - core},
            device_id_type=MESH,
        )

    def store(piece):
        return pltpu.make_async_copy(pair.at[piece], out_pieces.at[piece], store_sem.at[piece])

    def advance(piece, step):
        if step == 0:
            pair_copy(piece).wait_recv()

            def some(index, carry):
                shards = pl.ds(index * 4, 4)
                held[piece, shards] = held[piece, shards] + pair[piece, shards]
                return carry

            lax.fori_loop(0, SHARDS // 4, some, 0)
        else:
            copy(piece, step - 1).wait_recv()
            if halving < step <= bits:
                copy(piece, step - 1).wait_send()
            if step <= bits:
                add_level(piece, step - 1)
        if step < sends:
            copy(piece, step).start()
        else:
            store(piece).start()
            for earlier in early_sends:
                copy(piece, earlier).wait_send()
            pair_copy(piece).wait_send()

    early_sends = [step for step in range(sends - 1) if not halving <= step < bits]

    def offset_of(step):
        return LAG * step + (DELAY if step >= bits else 0)

    def tick(time, carry):
        for step in range(sends + 1):
            piece = time - offset_of(step)

            @pl.when((piece >= 0) & (piece < pieces))
            def _():
                advance(piece, step)

        return carry

    def ticks(first, amount):
        lax.fori_loop(first, first + amount, tick, 0)

    def send_pairs(first, amount):
        def one(piece, carry):
            pair_copy(piece).start()
            return carry

        lax.fori_loop(first, first + amount, one, 0)

    def load(source, target, place):
        return pltpu.make_async_copy(source, target, load_sem.at[place])

    loads = [
        load(tokens.at[my_rows], x_s, 0),
        load(cotangent.at[my_rows], dy_s, 1),
        load(w_query, wqkv.at[0, :, pl.ds(0, local)], 2),
        load(w_key, wqkv.at[0, :, pl.ds(local, local)], 3),
        load(w_value, wqkv.at[0, :, pl.ds(2 * local, local)], 4),
        load(w_out, wo.at[pl.ds(0, local)], 5),
        load(w_in, wi.at[0], 6),
        load(w_back, wb.at[0], 7),
    ]
    for item in loads:
        item.start()

    barrier = pltpu.get_barrier_semaphore()
    pl.semaphore_signal(barrier, inc=1, device_id={"tensor": 1 - core}, device_id_type=MESH)
    for bit in range(bits):
        mine = lax.rem(lax.div(me, 1 << bit), 2)
        pl.semaphore_signal(
            barrier,
            inc=1,
            device_id={"dp": me + (1 - 2 * mine) * (1 << bit)},
            device_id_type=MESH,
        )
    pl.semaphore_wait(barrier, bits + 1)

    def to_partner(source, target, place):
        return pltpu.make_async_remote_copy(
            src_ref=source,
            dst_ref=target,
            send_sem=weight_send.at[place],
            recv_sem=weight_recv.at[place],
            device_id={"tensor": 1 - core},
            device_id_type=MESH,
        )

    gathers = [
        to_partner(b_query, bias_q, 0),
        to_partner(b_value, bias_v, 1),
        to_partner(b_in, bias_i, 2),
        to_partner(w_query, wqkv.at[1, :, pl.ds(0, local)], 3),
        to_partner(w_key, wqkv.at[1, :, pl.ds(local, local)], 4),
        to_partner(w_value, wqkv.at[1, :, pl.ds(2 * local, local)], 5),
        to_partner(w_out, wo.at[pl.ds(local, local)], 6),
        to_partner(w_in, wi.at[1], 7),
        to_partner(w_back, wb.at[1], 8),
    ]
    for item in gathers:
        item.start()

    vec[...] = jnp.zeros_like(vec)
    vec_other[...] = jnp.zeros_like(vec_other)
    ffn[...] = jnp.zeros_like(ffn)
    dn2[...] = jnp.zeros_like(dn2)

    small = 256
    loads[0].wait()

    def first_norm(tile, carry):
        rows = pl.ds(pl.multiple_of(tile * small, small), small)
        unit, rstd = norm_parts(x_s[rows].astype(F32))
        normed[rows] = (unit * row_of(gain_attn) + row_of(shift_attn)).astype(BF16)
        return carry

    lax.fori_loop(0, SEQ // small, first_norm, 0)

    for half in range(2):
        if half == 0:
            for item in loads[2:5]:
                item.wait()
            bias_query, bias_value = b_query, b_value
        else:
            for item in gathers[0:2] + gathers[3:6]:
                item.wait_recv()
            bias_query, bias_value = bias_q, bias_v
        qkv[half, :, 0:local] = (
            matmul(normed[...], wqkv[half, :, 0:local]) + row_of(bias_query)
        ).astype(BF16)
        qkv[half, :, local : 2 * local] = matmul(
            normed[...], wqkv[half, :, local : 2 * local]
        ).astype(BF16)
        qkv[half, :, 2 * local : 3 * local] = (
            matmul(normed[...], wqkv[half, :, 2 * local : 3 * local]) + row_of(bias_value)
        ).astype(BF16)

    pairs_half = local // LANES
    scale = HEAD ** (-0.5)
    lane = lax.broadcasted_iota(jnp.int32, (1, LANES), 1)
    masks = [
        jnp.where((lane >= part * HEAD) & (lane < (part + 1) * HEAD), 1.0, 0.0).astype(BF16)
        for part in range(LANES // HEAD)
    ]
    queries = 128

    def columns(index, group):
        return pl.ds(pl.multiple_of(group * local + index * LANES, LANES), LANES)

    def attend(index, carry):
        half, place = lax.div(index, pairs_half), lax.rem(index, pairs_half)
        key = qkv[half, :, columns(place, 1)]
        value = qkv[half, :, columns(place, 2)]
        total = None
        for part, mask in enumerate(masks):
            for tile in range(SEQ // queries):
                rows = slice(tile * queries, (tile + 1) * queries)
                query = qkv[half, rows, columns(place, 0)] * (mask * scale).astype(BF16)
                scores = matmul_right(key, query)
                top = jnp.max(scores, axis=0, keepdims=True)
                expo = jnp.exp(scores - top)
                amount = jnp.sum(expo, axis=0, keepdims=True)
                lse[index * 2 + part, :, rows] = top + jnp.log(amount)
                probs_t[part, :, rows] = (expo * (1.0 / amount)).astype(BF16)
            term = matmul_left(probs_t[part], value * mask)
            total = term if total is None else total + term
        mixed[:, pl.ds(pl.multiple_of(index * LANES, LANES), LANES)] = total.astype(BF16)
        return carry

    lax.fori_loop(0, 2 * pairs_half, attend, 0)

    loads[5].wait()
    gathers[6].wait_recv()
    hidden[...] = matmul(mixed[...], wo[...])

    def second_norm(tile, carry):
        rows = pl.ds(pl.multiple_of(tile * small, small), small)
        whole = x_s[rows].astype(F32) + (hidden[rows] + row_of(b_out))
        hidden[rows] = whole
        unit, rstd = norm_parts(whole)
        normed2[rows] = (unit * row_of(gain_ffn) + row_of(shift_ffn)).astype(BF16)
        return carry

    lax.fori_loop(0, SEQ // small, second_norm, 0)
    flip2[...] = normed2[...].T

    loads[1].wait()
    loads[6].wait()
    loads[7].wait()
    gathers[2].wait_recv()
    gathers[7].wait_recv()
    gathers[8].wait_recv()
    ones = jnp.ones((16, SEQ), BF16)
    fine = 32
    tall = 512

    def hand_in(target, first, grad, kind, part):
        wide = 2 * LANES
        if kind == "in":
            for side in range(2):
                target[first + 2 * part + side] = (
                    grad[:, side * LANES : (side + 1) * LANES]
                    .astype(BF16)
                    .reshape(SHARDS, ROWS, LANES)
                )
        else:
            blocks = grad.shape[0] // (ROWS * SHARDS // 2)
            for block in range(blocks):
                rows = slice(block * ROWS * SHARDS // 2, (block + 1) * ROWS * SHARDS // 2)
                for side in range(2):
                    target[
                        first + (width // wide) * block + part,
                        side * (SHARDS // 2) : (side + 1) * (SHARDS // 2),
                    ] = (
                        grad[rows, side * LANES : (side + 1) * LANES]
                        .astype(BF16)
                        .reshape(SHARDS // 2, ROWS, LANES)
                    )

    def feed(chunk, half, slots):
        begin = pl.multiple_of(chunk * width, width)
        units = pl.ds(begin, width)
        bias_row = b_in if half == 0 else bias_i
        target = held if half == 0 else other
        first = chunk * size.per_chunk

        def rows_tile(tile, carry):
            rows = pl.ds(pl.multiple_of(tile * tall, tall), tall)
            wide_a[...] = matmul(normed2[rows], wi[half, :, units])
            wide_b[...] = matmul_right(dy_s[rows], wb[half, units, :])

            def inner(step, carry):
                piece = pl.ds(pl.multiple_of(step * fine, fine), fine)
                there = pl.ds(pl.multiple_of(tile * tall + step * fine, fine), fine)
                pre = wide_a[piece] + bias_row[units].reshape(1, -1)
                phi = 0.5 * (1.0 + lax.erf(pre * 0.7071067811865476))
                act[there] = (pre * phi).astype(BF16)
                slope = phi + pre * jnp.exp(-0.5 * pre * pre) * 0.3989422804014327
                dpre[there] = (wide_b[piece] * slope).astype(BF16)
                return carry

            lax.fori_loop(0, tall // fine, inner, 0)
            return carry

        lax.fori_loop(0, SEQ // tall, rows_tile, 0)
        flip[...] = act[...].T
        slots(0)
        for part in range(width // 256):
            cols = slice(part * 256, (part + 1) * 256)
            hand_in(target, first, matmul(flip2[...], dpre[:, cols]), "in", part)
        for part in range(width // 256):
            cols = slice(part * 256, (part + 1) * 256)
            hand_in(target, first + size.block, matmul(flip[...], dy_s[:, cols]), "out", part)
        slots(1)
        if half == 0:
            slots(2)
        ffn[...] += matmul(act[...], wb[half, units, :])
        dn2[...] += matmul_right(dpre[...], wi[half, :, units])
        sums = matmul(ones, dpre[...])[0:1]
        (vec if half == 0 else vec_other)[pl.ds(7 + chunk, 1)] = sums

    def feed_both(chunk, carry):
        def slots(offset, half):
            def place(index):
                first = HEAD_START + (chunk - 1) * 4 * EACH + (offset + index) * EACH
                if index == 1 and half == 1:
                    send_pairs(chunk * size.per_chunk, size.per_chunk)
                if index == 2:
                    lax.fori_loop(0, jnp.where(chunk > 0, 0, HEAD_START), tick, 0)
                else:
                    lax.fori_loop(first, jnp.where(chunk > 0, first + EACH, first), tick, 0)

            return place

        feed(chunk, 1, slots(0, 1))
        feed(chunk, 0, slots(2, 0))
        return carry

    lax.fori_loop(0, size.chunks, feed_both, 0)
    time = HEAD_START + (size.chunks - 1) * 4 * EACH

    tiny = 128

    def second_back(tile, carry):
        sum_gain, sum_shift, sum_out = carry
        rows = pl.ds(pl.multiple_of(tile * tiny, tiny), tiny)
        whole = hidden[rows]
        act[rows] = (whole + (ffn[rows] + row_of(b_back))).astype(BF16)
        unit, rstd = norm_parts(whole)
        grad = dn2[rows]
        dhidden = dy_s[rows].astype(F32) + norm_back(grad * row_of(gain_ffn), unit, rstd)
        dn2[rows] = dhidden
        rounded = dhidden.astype(BF16)
        dattn[rows] = rounded
        return (
            sum_gain + fold(grad * unit),
            sum_shift + fold(grad),
            sum_out + fold(rounded.astype(F32)),
        )

    zero = jnp.zeros((8, width), F32)
    sum_gain, sum_shift, sum_out = lax.fori_loop(
        0, SEQ // tiny, second_back, (zero, zero, zero)
    )

    def both(row, value):
        vec[row : row + 1] = value
        vec_other[row : row + 1] = value

    both(0, jnp.sum(sum_out, axis=0, keepdims=True))
    both(1, matmul(ones, dy_s[...])[0:1])
    both(4, jnp.sum(sum_gain, axis=0, keepdims=True))
    both(5, jnp.sum(sum_shift, axis=0, keepdims=True))

    def row_copies(source, target, place):
        return (
            pltpu.make_async_copy(source, target.at[my_rows], row_sem.at[place]),
            pltpu.make_async_remote_copy(
                src_ref=source,
                dst_ref=target.at[my_rows],
                send_sem=row_send.at[place],
                recv_sem=row_recv.at[place],
                device_id={"tensor": 1 - core},
                device_id_type=MESH,
            ),
        )

    result_copies = row_copies(act, out_rows, 0)
    for item in result_copies:
        item.start()
    ticks(time, NORM_TICKS)
    time += NORM_TICKS

    flip[...] = mixed[...].T
    for part in range(width // 256):
        cols = slice(part * 256, (part + 1) * 256)
        grad = matmul(flip[...], dattn[:, cols])
        hand_in(held, size.first_out, grad[0:local], "out", part)
        hand_in(other, size.first_out, grad[local:], "out", part)
    send_pairs(size.first_out, size.first_qkv - size.first_out)
    dmixed[...] = matmul_right(dattn[...], wo[...]).astype(BF16)
    ticks(time, OUT_TICKS)
    time += OUT_TICKS

    def attend_back(index, carry):
        half, place = lax.div(index, pairs_half), lax.rem(index, pairs_half)
        here = pl.ds(pl.multiple_of(index * LANES, LANES), LANES)
        key = qkv[half, :, columns(place, 1)]
        value = qkv[half, :, columns(place, 2)]
        dquery, dkey, dvalue = None, None, None
        for part, mask in enumerate(masks):
            for tile in range(SEQ // queries):
                rows = slice(tile * queries, (tile + 1) * queries)
                query = qkv[half, rows, columns(place, 0)] * (mask * scale).astype(BF16)
                scores = matmul_right(key, query)
                probs = jnp.exp(scores - lse[index * 2 + part, :, rows])
                dprobs = matmul_right(value, dmixed[rows, here] * mask)
                inner = jnp.sum(dprobs * probs, axis=0, keepdims=True)
                probs_t[part, :, rows] = probs.astype(BF16)
                dscores_t[part, :, rows] = (probs * (dprobs - inner)).astype(BF16)
            query = qkv[half, :, columns(place, 0)] * (mask * scale).astype(BF16)
            terms = (
                matmul_left(dscores_t[part], key * mask),
                matmul(dscores_t[part], query),
                matmul(probs_t[part], dmixed[:, here] * mask),
            )
            if dquery is None:
                dquery, dkey, dvalue = terms
            else:
                dquery, dkey, dvalue = dquery + terms[0], dkey + terms[1], dvalue + terms[2]
        qkv[half, :, columns(place, 0)] = (dquery * scale).astype(BF16)
        qkv[half, :, columns(place, 1)] = dkey.astype(BF16)
        qkv[half, :, columns(place, 2)] = dvalue.astype(BF16)
        ticks(time + index * PAIR_TICKS, PAIR_TICKS)
        return carry

    lax.fori_loop(0, 2 * pairs_half, attend_back, 0)
    time += 2 * pairs_half * PAIR_TICKS

    flip[...] = normed[...].T
    for half in (1, 0):
        target = held if half == 0 else other
        for part in range(3 * local // LANES):
            cols = slice(part * LANES, (part + 1) * LANES)
            grad = matmul(flip[...], qkv[half, :, cols])
            target[size.first_qkv + part] = grad.astype(BF16).reshape(SHARDS, ROWS, LANES)
        if half == 1:
            send_pairs(size.first_qkv, size.pieces - size.first_qkv)
        amount = min(QKV_TICKS, size.first_qkv - time) if half == 1 else QKV_TICKS + 1
        ticks(time, amount)
        time += amount
    for half in range(2):
        table = vec if half == 0 else vec_other
        table[6:7, 0:local] = matmul(ones, qkv[half, :, 0:local])[0:1]
        table[6:7, local : 2 * local] = matmul(ones, qkv[half, :, 2 * local : 3 * local])[0:1]
    hidden[...] = matmul_right(qkv[0], wqkv[0])
    hidden[...] += matmul_right(qkv[1], wqkv[1])
    ticks(time, QKV_TICKS)
    time += QKV_TICKS

    def first_back(tile, carry):
        sum_gain, sum_shift = carry
        rows = pl.ds(pl.multiple_of(tile * tiny, tiny), tiny)
        unit, rstd = norm_parts(x_s[rows].astype(F32))
        grad = hidden[rows]
        ffn[rows] = dn2[rows] + norm_back(grad * row_of(gain_attn), unit, rstd)
        return sum_gain + fold(grad * unit), sum_shift + fold(grad)

    sum_gain, sum_shift = lax.fori_loop(0, SEQ // tiny, first_back, (zero, zero))
    both(2, jnp.sum(sum_gain, axis=0, keepdims=True))
    both(3, jnp.sum(sum_shift, axis=0, keepdims=True))
    grad_copies = row_copies(ffn, out_grad, 1)
    for item in grad_copies:
        item.start()

    def vector_copy(step):
        if step == 0:
            source, partner = vec_other, {"tensor": 1 - core}
        else:
            bit = lax.rem(lax.div(me, 1 << (step - 1)), 2)
            source, partner = vec, {"dp": me + (1 - 2 * bit) * (1 << (step - 1))}
        return pltpu.make_async_remote_copy(
            src_ref=source,
            dst_ref=vec_landed.at[step],
            send_sem=vec_send.at[step],
            recv_sem=vec_recv.at[step],
            device_id=partner,
            device_id_type=MESH,
        )

    for step in range(bits + 1):
        vector_copy(step).start()
        ticks(time, 3)
        time += 3
        vector_copy(step).wait()
        vec[...] += vec_landed[step]
    vector_store = pltpu.make_async_copy(vec, out_vectors, row_sem.at[2])
    vector_store.start()
    ticks(time, pieces + offset_of(sends) - time)

    def finish(piece, carry):
        copy(piece, sends - 1).wait_send()
        store(piece).wait()
        return carry

    lax.fori_loop(0, pieces, finish, 0)
    for item in gathers:
        item.wait_send()
    for local_copy, remote_copy in (result_copies, grad_copies):
        local_copy.wait()
        remote_copy.wait()
    vector_store.wait()


def run_layer(size, arrays, vectors):
    width, local, hidden = size.width, size.local, size.hidden
    rows = arrays[0].shape[0]
    steps = size.sends
    rank = pltpu.SemaphoreType
    any_space = pl.BlockSpec(memory_space=pl.ANY)
    in_vmem = pl.BlockSpec(memory_space=pltpu.VMEM)
    piece_shape = (size.pieces, SHARDS, ROWS, LANES)
    scratch = [
        pltpu.VMEM((2, width, 3 * local), BF16),
        pltpu.VMEM((2 * local, width), BF16),
        pltpu.VMEM((2, width, hidden), BF16),
        pltpu.VMEM((2, hidden, width), BF16),
        pltpu.VMEM((local,), F32),
        pltpu.VMEM((local,), F32),
        pltpu.VMEM((hidden,), F32),
        pltpu.VMEM((SEQ, width), BF16),
        pltpu.VMEM((SEQ, width), BF16),
        pltpu.VMEM((SEQ, width), BF16),
        pltpu.VMEM((2, SEQ, 3 * local), BF16),
        pltpu.VMEM((SEQ, width), BF16),
        pltpu.VMEM((2 * local // HEAD, 1, SEQ), F32),
        pltpu.VMEM((SEQ, width), F32),
        pltpu.VMEM((SEQ, width), BF16),
        pltpu.VMEM((width, SEQ), BF16),
        pltpu.VMEM((SEQ, width), F32),
        pltpu.VMEM((SEQ, width), F32),
        pltpu.VMEM((SEQ, width), BF16),
        pltpu.VMEM((SEQ, width), BF16),
        pltpu.VMEM((width, SEQ), BF16),
        pltpu.VMEM((SEQ, width), F32),
        pltpu.VMEM((SEQ, width), F32),
        pltpu.VMEM((SEQ, width), BF16),
        pltpu.VMEM((SEQ, width), BF16),
        pltpu.VMEM((LANES // HEAD, SEQ, SEQ), BF16),
        pltpu.VMEM((LANES // HEAD, SEQ, SEQ), BF16),
        pltpu.VMEM(piece_shape, BF16),
        pltpu.VMEM(piece_shape, BF16),
        pltpu.VMEM(piece_shape, BF16),
        pltpu.VMEM((size.pieces, size.landing, ROWS, LANES), BF16),
        pltpu.VMEM((16, width), F32),
        pltpu.VMEM((16, width), F32),
        pltpu.VMEM((size.bits + 1, 16, width), F32),
        rank.DMA((8,)),
        rank.DMA((9,)),
        rank.DMA((9,)),
        rank.DMA((size.pieces,)),
        rank.DMA((size.pieces,)),
        rank.DMA((size.pieces, steps)),
        rank.DMA((size.pieces, steps)),
        rank.DMA((size.pieces,)),
        rank.DMA((size.bits + 1,)),
        rank.DMA((size.bits + 1,)),
        rank.DMA((2,)),
        rank.DMA((2,)),
        rank.DMA((3,)),
    ]
    return pl.pallas_call(
        functools.partial(layer_kernel, size),
        out_shape=(
            jax.ShapeDtypeStruct((rows, width), BF16),
            jax.ShapeDtypeStruct((rows, width), F32),
            jax.ShapeDtypeStruct(piece_shape, BF16),
            jax.ShapeDtypeStruct((16, width), F32),
        ),
        in_specs=[any_space] * len(arrays) + [in_vmem] * len(vectors),
        out_specs=(any_space,) * 4,
        scratch_shapes=scratch,
        compiler_params=pltpu.CompilerParams(
            collective_id=0, has_side_effects=True, vmem_limit_bytes=67043328
        ),
        name="layer",
    )(*arrays, *vectors)


def unpack_kernel(size, pieces, vectors_in, rows_in, grad_in, *refs):
    g_wq, g_wk, g_wv, g_wo, g_wi, g_wb, rows_end, grad_end = refs[:8]
    rows_out = refs[8:17]
    held, s_in, s_back, s_qkv, s_out, vectors, rows, grad, sem, out_sem, side_sem = refs[17:]
    width, local = size.width, size.local
    wide = 2 * LANES
    half_rows = ROWS * SHARDS // 2
    spans = []
    for chunk in range(size.chunks):
        first = chunk * size.per_chunk
        spans.append((first, size.block))
        spans.append((first + size.block, size.block))
    spans.append((size.first_out, size.first_qkv - size.first_out))
    for index in range(3):
        spans.append((size.first_qkv + index * local // LANES, local // LANES))
    copies = []
    for index, (first, amount) in enumerate(spans):
        item = pltpu.make_async_copy(
            pieces.at[pl.ds(first, amount)], held.at[pl.ds(first, amount)], sem.at[index]
        )
        item.start()
        copies.append(item)
    sides = [
        pltpu.make_async_copy(source, target, side_sem.at[index])
        for index, (source, target) in enumerate(
            ((vectors_in, vectors), (rows_in, rows), (grad_in, grad))
        )
    ]
    for item in sides:
        item.start()
    sides[0].wait()
    for ref, row, begin, amount in zip(
        rows_out,
        (6, 6, 0, 7, 1, 2, 3, 4, 5),
        (0, local, 0, 0, 0, 0, 0, 0, 0),
        (local, local, width, width, width, width, width, width, width),
    ):
        for chunk in range(ref.shape[0] // amount):
            ref[chunk * amount : (chunk + 1) * amount] = vectors[
                row + chunk, begin : begin + amount
            ]

    outs = []

    def put(source, target):
        item = pltpu.make_async_copy(source, target, out_sem.at[len(outs)])
        item.start()
        outs.append(item)

    def columns(first, amount, target, begin):
        for index in range(amount):
            target[:, begin + index * LANES : begin + (index + 1) * LANES] = (
                held[first + index].reshape(SHARDS * ROWS, LANES).astype(F32)
            )

    def blocks(first, rows, target, begin):
        for block in range(rows // half_rows):
            for part in range(width // wide):
                for side in range(2):
                    value = held[
                        first + block * (width // wide) + part,
                        side * (SHARDS // 2) : (side + 1) * (SHARDS // 2),
                    ]
                    target[
                        begin + block * half_rows : begin + (block + 1) * half_rows,
                        part * wide + side * LANES : part * wide + (side + 1) * LANES,
                    ] = value.reshape(half_rows, LANES).astype(F32)

    at = 0
    for chunk in range(size.chunks):
        first = chunk * size.per_chunk
        copies[at].wait()
        columns(first, size.block, s_in.at[chunk], 0)
        put(s_in.at[chunk], g_wi.at[:, pl.ds(chunk * width, width)])
        copies[at + 1].wait()
        blocks(first + size.block, width, s_back, chunk * width)
        put(
            s_back.at[pl.ds(chunk * width, width)],
            g_wb.at[pl.ds(chunk * width, width)],
        )
        at += 2
    copies[at].wait()
    blocks(size.first_out, local, s_out, 0)
    put(s_out, g_wo)
    at += 1
    for index, target in enumerate((g_wq, g_wk, g_wv)):
        copies[at].wait()
        columns(size.first_qkv + index * local // LANES, local // LANES, s_qkv.at[index], 0)
        put(s_qkv.at[index], target)
        at += 1
    sides[1].wait()
    put(rows, rows_end)
    sides[2].wait()
    put(grad, grad_end)
    for item in outs:
        item.wait()


def unpack(size, pieces, vectors, block_rows, grad_rows):
    width, local, hidden = size.width, size.local, size.hidden
    any_space = pl.BlockSpec(memory_space=pl.ANY)
    in_vmem = pl.BlockSpec(memory_space=pltpu.VMEM)
    matrices = [(width, local)] * 3 + [(local, width), (width, hidden), (hidden, width)]
    rows = [local, local, width, hidden, width, width, width, width, width]
    transfers = 2 * size.chunks + 6
    return pl.pallas_call(
        functools.partial(unpack_kernel, size),
        out_shape=tuple(jax.ShapeDtypeStruct(shape, F32) for shape in matrices)
        + tuple(jax.ShapeDtypeStruct(item.shape, item.dtype) for item in (block_rows, grad_rows))
        + tuple(jax.ShapeDtypeStruct((amount,), F32) for amount in rows),
        in_specs=[any_space] * 4,
        out_specs=(any_space,) * 8 + (in_vmem,) * 9,
        scratch_shapes=[
            pltpu.VMEM(pieces.shape, BF16),
            pltpu.VMEM((size.chunks, width, width), F32),
            pltpu.VMEM((hidden, width), F32),
            pltpu.VMEM((3, width, local), F32),
            pltpu.VMEM((local, width), F32),
            pltpu.VMEM(vectors.shape, F32),
            pltpu.VMEM(block_rows.shape, BF16),
            pltpu.VMEM(grad_rows.shape, F32),
            pltpu.SemaphoreType.DMA((transfers,)),
            pltpu.SemaphoreType.DMA((transfers,)),
            pltpu.SemaphoreType.DMA((3,)),
        ],
        compiler_params=pltpu.CompilerParams(vmem_limit_bytes=67043328),
        name="unpack",
    )(pieces, vectors, block_rows, grad_rows)


def on_device(
    tokens,
    cotangent,
    w_query,
    b_query,
    w_key,
    w_value,
    b_value,
    w_out,
    b_out,
    w_in,
    b_in,
    w_back,
    b_back,
    gain_attn,
    shift_attn,
    gain_ffn,
    shift_ffn,
):
    size = Sizes(lax.axis_size("dp"), tokens, w_query, w_in)
    assert tokens.shape[0] == SEQ * lax.axis_size("tensor") and lax.axis_size("tensor") == 2
    assert size.count == 1 << size.bits and size.width == SHARDS * ROWS
    vectors = (
        b_query,
        b_value,
        b_out,
        b_in,
        b_back,
        gain_attn,
        shift_attn,
        gain_ffn,
        shift_ffn,
    )
    rows, grad_rows, pieces, sums = run_layer(
        size,
        (tokens, cotangent, w_query, w_key, w_value, w_out, w_in, w_back),
        vectors,
    )
    outs = unpack(size, pieces, sums, rows, grad_rows)
    g_wq, g_wk, g_wv, g_wo, g_wi, g_wb = outs[:6]
    g_bq, g_bv, g_bo, g_bi, g_bb, g_ga, g_sa, g_gf, g_sf = outs[8:]
    return (
        *outs[6:8],
        g_wq,
        g_bq,
        g_wk,
        g_wv,
        g_bv,
        g_wo,
        g_bo,
        g_wi,
        g_bi,
        g_wb,
        g_bb,
        g_ga,
        g_sa,
        g_gf,
        g_sf,
    )


def solution(mesh):
    columns, rows, vector, whole = P(None, "tensor"), P("tensor", None), P("tensor"), P()
    weights = (
        columns,
        vector,
        columns,
        columns,
        vector,
        rows,
        whole,
        columns,
        vector,
        rows,
        whole,
        whole,
        whole,
        whole,
        whole,
    )
    data = (P("dp", None), P("dp", None))
    return jax.shard_map(
        on_device, mesh=mesh, in_specs=data + weights, out_specs=data + weights, check_vma=False
    )
```
